512 devices in a mesh: cam: 128 (over y, z, core), proj: 4 (over x).
Axes of the slice: x: 4, y: 8, z: 8, core: 2. Of those that a mesh axis runs over, the one named last changes fastest.
Arguments:
- transport: bfloat16 [65536, 16384], P('cam', 'proj'), may hold values from -0.09375 to 0.09375
- test_panel: bfloat16 [16384, 32], P(('proj', 'cam')), may hold values from -6 to 6
Outputs:
- basis: float32 [65536, 32], P('cam')
- coimage: float32 [16384, 32], P(('proj', 'cam'))
The draws below stay inside these ranges and needn't reach their ends.
All inputs are finite; a program needn't handle non-finite values.
Results may differ from the reference program's by a relative error of at most 0.0027.
Values may be sent and summed in bfloat16 or wider, within the bound.
No kernel may reach another device: no remote copies, remote signals or barrier semaphores. Data moves between devices by JAX's collectives and lax.ppermute only.
A program may use at most 64 MiB of HBM per device.

```python
import jax
import jax.numpy as jnp
from jax import lax

SLAB = 16384
RANK = 32
ITERS = 2
ROWS = 65536


def spiked(values, rng, source, target, shards_of, factor):
    owner, partner = [(jnp.arange(values.shape[axis_at]) // (values.shape[axis_at] // shards_of)).reshape([-1 if axis == axis_at else 1 for axis in range(values.ndim)]) for axis_at in (source, target)]
    chosen = jax.random.permutation(rng, shards_of)[partner]
    strong = (owner == chosen) | (owner == (partner + shards_of // 2) % shards_of)
    return jnp.where(strong, factor * values, values)


def steps_of(rng, shape, shards, low, high):
    factor_of = 1.0
    for dim, shards_of in shards:
        draws = jax.random.uniform(jax.random.fold_in(jax.random.fold_in(rng, 6), dim), (shards_of,), jnp.float32, low / len(shards), high / len(shards))
        factor_of = factor_of * jnp.repeat(jnp.exp(draws), shape[dim] // shards_of).reshape((-1,) + (1,) * (len(shape) - 1 - dim))
    return factor_of


def bell_draw(stream_key, extent, width, limit, cuts=(), dtype=jnp.bfloat16):
    result = jax.random.normal(stream_key, extent, jnp.float32) * width
    if len(cuts) > 0:
        result = steps_of(stream_key, extent, cuts, -0.22, 0.18) * result
    return jnp.clip(result, min=-limit, max=limit).astype(dtype)


def gaussian_with(stream_key, shape, spread, limit, cuts, heavy, held_as=jnp.bfloat16):
    entries = spread * jax.random.normal(stream_key, shape, jnp.float32)
    if cuts:
        entries = entries * steps_of(stream_key, shape, cuts, -0.22, 0.18)
    return jnp.clip(spiked(entries, jax.random.fold_in(stream_key, 3), *heavy), -limit, limit).astype(held_as)


def setup_inputs(seed: int = 0) -> dict:
    seeds = jax.random.split(jax.random.key(seed), 3)
    return {
        "transport": gaussian_with(seeds[0], (ROWS, SLAB), ROWS ** -0.5, 0.09375, ((0, 128), (1, 4)), (0, 1, 128, 5.5)),
        "test_panel": bell_draw(seeds[1], (SLAB, RANK), 1.0, 6.0, ((0, 512),)),
    }


def orthonormal(block, count):
    gram = jnp.dot(block.T.astype(jnp.float32), block.astype(jnp.float32), precision=lax.Precision.HIGHEST, preferred_element_type=jnp.float32) / count
    lower = jnp.linalg.cholesky(gram)
    return jax.scipy.linalg.solve_triangular(lower, block.T, lower=True).T

def reference(transport, test_panel):
    panel = test_panel
    basis = None
    coimage = None
    for step in range(ITERS):
        sketch = jnp.dot(transport.astype(jnp.float32), panel.astype(jnp.float32), preferred_element_type=jnp.float32)
        basis = orthonormal(sketch, ROWS)
        basis_low = basis.astype(jnp.bfloat16)
        coimage = jnp.dot(transport.T.astype(jnp.float32), basis_low.astype(jnp.float32), preferred_element_type=jnp.float32)
        if step + 1 < ITERS:
            panel = coimage.astype(jnp.bfloat16)
    return (basis, coimage)
```

```python
import jax
import jax.numpy as jnp
import numpy as np
from jax import lax
from jax.sharding import Mesh
from jax.sharding import PartitionSpec as P

ITERS = 2
CHIPS = ("y", "z")
HIGHEST = lax.Precision.HIGHEST


def pack(square):
    return square.reshape(4, 8, 32).transpose(1, 0, 2).reshape(8, 128)


def unpack(tile):
    return tile.reshape(8, 4, 32).transpose(1, 0, 2).reshape(32, 32)


def gather(tile):
    other = lax.ppermute(tile, "core", [(0, 1), (1, 0)])
    first = lax.axis_index("core") == 0
    pair = jnp.concatenate([jnp.where(first, tile, other), jnp.where(first, other, tile)])
    chips = lax.axis_size(CHIPS)
    copies = jnp.broadcast_to(pair, (chips,) + pair.shape)
    return lax.all_to_all(copies, CHIPS, 0, 0).reshape(2 * chips, 8, 128)


def sum_over_x(block):
    copies = jnp.broadcast_to(block, (lax.axis_size("x"),) + block.shape)
    return jnp.sum(lax.all_to_all(copies, "x", 0, 0), axis=0)


def reduce_tiles(tiles, gram):
    chips = lax.axis_size(CHIPS)
    halves = tiles.reshape(chips, 2, 8, 128).transpose(1, 0, 2, 3)
    grams = jnp.broadcast_to(gram, (2, 1, 8, 128))
    half = jnp.sum(lax.all_to_all(jnp.concatenate([halves, grams], axis=1), "core", 0, 0), axis=0)
    message = jnp.concatenate(
        [half[:chips], jnp.broadcast_to(half[chips:], (chips, 8, 128))], axis=1
    )
    total = jnp.sum(lax.all_to_all(message, CHIPS, 0, 0), axis=0)
    return total[:8], total[8:]


def inverse_factor(gram):
    lower = jnp.linalg.cholesky(gram)
    eye = jnp.eye(gram.shape[0], dtype=gram.dtype)
    return jax.scipy.linalg.solve_triangular(lower, eye, lower=True).T


def on_device(transport, test_panel):
    total_rows = transport.shape[0] * lax.axis_size(("y", "z", "core"))
    tile = pack(test_panel)
    basis = None
    for step in range(ITERS):
        tiles = gather(tile)
        panel = tiles.reshape(-1, 8, 4, 32).transpose(0, 2, 1, 3).reshape(-1, 32)
        partial = jnp.dot(transport, panel, preferred_element_type=jnp.float32)
        packed = partial.reshape(4, 128, 32).transpose(1, 0, 2).reshape(128, 128)
        sketch = sum_over_x(packed).reshape(128, 4, 32).transpose(1, 0, 2).reshape(512, 32)
        gram = jnp.dot(sketch.T, sketch, precision=HIGHEST, preferred_element_type=jnp.float32)
        high = sketch.astype(jnp.bfloat16)
        low = (sketch - high.astype(jnp.float32)).astype(jnp.bfloat16)
        both = lax.dot_general(
            transport,
            jnp.concatenate([high, low], axis=1),
            (((0,), (0,)), ((), ())),
            preferred_element_type=jnp.float32,
        )
        product = both[:, :32] + both[:, 32:]
        pieces = product.reshape(-1, 4, 8, 32).transpose(0, 2, 1, 3).reshape(-1, 8, 128)
        piece, gram = reduce_tiles(pieces, pack(gram))
        inverse = inverse_factor(unpack(gram) / total_rows)
        coimage = jnp.dot(unpack(piece), inverse, precision=HIGHEST)
        if step + 1 < ITERS:
            tile = pack(coimage.astype(jnp.bfloat16))
        else:
            basis = jnp.dot(sketch, inverse, precision=HIGHEST)
    return (basis, coimage)


def solution(mesh):
    sizes = {"cam": (("y", 8), ("z", 8), ("core", 2)), "proj": (("x", 4),)}
    names = [name for axis in mesh.axis_names for name, _ in sizes[axis]]
    shape = [size for axis in mesh.axis_names for _, size in sizes[axis]]
    fine = Mesh(np.asarray(mesh.devices).reshape(shape), names)
    rows = ("y", "z", "core")
    return jax.shard_map(
        on_device,
        mesh=fine,
        in_specs=(P(rows, "x"), P(("x",) + rows, None)),
        out_specs=(P(rows, None), P(("x",) + rows, None)),
        check_vma=False,
    )
```

```python
import functools

import jax
import jax.numpy as jnp
import numpy as np
from jax import lax
from jax.experimental import pallas as pl
from jax.experimental.pallas import tpu as pltpu
from jax.sharding import Mesh
from jax.sharding import PartitionSpec as P

CHIPS = ("y", "z")
RANK = 32
HIGHEST = lax.Precision.HIGHEST
F32 = jnp.float32
BF16 = jnp.bfloat16
VMEM = pl.BlockSpec(memory_space=pltpu.VMEM)
NT = (((1,), (1,)), ((), ()))
TN = (((0,), (0,)), ((), ()))


def kernel_call(body, outs, flops, moved, *args):
    return pl.pallas_call(
        body,
        out_shape=outs,
        in_specs=[VMEM] * len(args),
        out_specs=jax.tree.map(lambda _: VMEM, outs),
        compiler_params=pltpu.CompilerParams(vmem_limit_bytes=24 << 20),
        cost_estimate=pl.CostEstimate(flops=flops, bytes_accessed=moved, transcendentals=0),
    )(*args)


def lanes_of(shape):
    return lax.broadcasted_iota(jnp.int32, shape, len(shape) - 1)


def pack_square(square):
    lane = lanes_of((8, 128))
    out = jnp.where(lane < 32, square[0:8], 0.0)
    for q in range(1, 4):
        block = pltpu.roll(square[8 * q : 8 * q + 8], 32 * q, axis=1)
        out = jnp.where((lane >= 32 * q) & (lane < 32 * q + 32), block, out)
    return out


def unpack_square(tile):
    return jnp.concatenate([tile] + [pltpu.roll(tile, 128 - 32 * q, axis=1) for q in range(1, 4)])


def inverse_factor(gram):
    lane = lanes_of((RANK, 128))
    row = lax.broadcasted_iota(jnp.int32, (RANK, 128), 0)
    work = jnp.where(lane < RANK, gram, jnp.where(lane == row + RANK, 1.0, 0.0))
    pivots = jnp.ones((RANK, 128), F32)
    width = 8
    for start in range(0, RANK, width):
        columns = [
            jnp.broadcast_to(work[:, start + i : start + i + 1], (RANK, 128)) for i in range(width)
        ]
        for i in range(width):
            k = start + i
            pivot = jnp.broadcast_to(columns[i][k : k + 1], (RANK, 128))
            pivots = jnp.where(row == k, pivot, pivots)
            factor = jnp.where(row > k, columns[i] / pivot, 0.0)
            for later in range(i + 1, width):
                columns[later] = columns[later] - factor * columns[later][k : k + 1]
            work = work - factor * work[k : k + 1]
    return (work / jnp.sqrt(pivots))[:, RANK : 2 * RANK]


def first_sketch(tiles_ref, transport_ref, out_ref):
    chips, cols = tiles_ref.shape[0], transport_ref.shape[1]
    lane = lanes_of((16, 128))
    masks = [(lane >= 32 * q) & (lane < 32 * q + 32) for q in range(4)]
    total = jnp.zeros((transport_ref.shape[0], 128), F32)
    group = 8
    for start in range(0, chips, group):
        rows = []
        for chip in range(start, start + group):
            tile = tiles_ref[chip]
            rows += [jnp.where(mask, tile, jnp.zeros_like(tile)) for mask in masks]
        at = start * (cols // chips)
        total += jnp.dot(
            transport_ref[:, at : at + group * (cols // chips)],
            jnp.concatenate(rows),
            preferred_element_type=F32,
        )
    turned = total.T
    sketch = (turned[0:32] + turned[32:64]) + (turned[64:96] + turned[96:128])
    for copy in range(out_ref.shape[0]):
        out_ref[copy] = sketch


def next_sketch(panel_ref, transport_ref, out_ref):
    groups, _, width = panel_ref.shape
    sketch = jnp.zeros((RANK, transport_ref.shape[0]), F32)
    for g in range(groups):
        sketch += lax.dot_general(
            panel_ref[g],
            transport_ref[:, g * width : (g + 1) * width],
            NT,
            preferred_element_type=F32,
        )
    for copy in range(out_ref.shape[0]):
        out_ref[copy] = sketch


def product(parts_ref, transport_ref):
    sketch = (parts_ref[0] + parts_ref[1]) + (parts_ref[2] + parts_ref[3])
    gram = lax.dot_general(sketch, sketch, NT, precision=HIGHEST, preferred_element_type=F32)
    gram = jnp.concatenate([gram, jnp.zeros((RANK, 128 - RANK), F32)], axis=1)
    high = sketch.astype(BF16)
    low = (sketch - high.astype(F32)).astype(BF16)
    both = jnp.concatenate([high, low])

    def columns(at, width):
        out = jnp.dot(both, transport_ref[:, at : at + width], preferred_element_type=F32)
        return out[:RANK] + out[RANK:]

    return sketch, pack_square(gram), columns


def middle_product(parts_ref, transport_ref, out_ref):
    cores, groups, height, _ = out_ref.shape
    tiles = height // 8 - 1
    width = tiles // 4 * 128
    _, gram, columns = product(parts_ref, transport_ref)
    for core in range(cores):
        for g in range(groups):
            block = columns((core * groups + g) * width, width)
            for t in range(tiles):
                a, c = t % 4, t // 4
                out_ref[core, g, 8 * t : 8 * t + 8] = block[8 * a : 8 * a + 8, 128 * c : 128 * c + 128]
            out_ref[core, g, 8 * tiles : height] = gram


def last_product(parts_ref, transport_ref, out_ref, sketch_ref):
    cores, chips, _, _ = out_ref.shape
    sketch, gram, columns = product(parts_ref, transport_ref)
    sketch_ref[...] = sketch
    lane = lanes_of((8, 128))
    low_half, even = lane < 64, lane % 64 < 32
    for wide in range(chips // 8):
        block = columns(512 * wide, 512)
        for c in range(4):
            t = [block[8 * a : 8 * a + 8, 128 * c : 128 * c + 128] for a in range(4)]
            u = [None] * 4
            for a in (0, 1):
                u[a] = jnp.where(low_half, t[a], pltpu.roll(t[a + 2], 64, axis=1))
                u[a + 2] = jnp.where(low_half, pltpu.roll(t[a], 64, axis=1), t[a + 2])
            for a in (0, 2):
                v0 = jnp.where(even, u[a], pltpu.roll(u[a + 1], 32, axis=1))
                v1 = jnp.where(even, pltpu.roll(u[a], 96, axis=1), u[a + 1])
                for b, v in ((a, v0), (a + 1, v1)):
                    device = 16 * wide + 4 * c + b
                    out_ref[device % 2, device // 2, 0:8] = v
    for core in range(cores):
        for chip in range(chips):
            out_ref[core, chip, 8:16] = gram


def normalise(total_rows, sums_ref, out_ref):
    peers, height, _ = sums_ref.shape
    total = sums_ref[0]
    for p in range(1, peers):
        total = total + sums_ref[p]
    tiles = height // 8 - 1
    inverse = inverse_factor(unpack_square(total[8 * tiles :]) / total_rows)
    for c in range(tiles // 4):
        block = total[32 * c : 32 * c + 32]
        panel = jnp.dot(inverse, block, precision=HIGHEST, preferred_element_type=F32).astype(BF16)
        for copy in range(out_ref.shape[0]):
            out_ref[copy, :, 128 * c : 128 * c + 128] = panel


def finish(total_rows, sums_ref, sketch_ref, basis_ref, coimage_ref):
    total = sums_ref[0]
    for p in range(1, sums_ref.shape[0]):
        total = total + sums_ref[p]
    inverse = inverse_factor(unpack_square(total[8:16]) / total_rows)
    basis_ref[...] = jnp.dot(
        inverse, sketch_ref[...], precision=HIGHEST, preferred_element_type=F32
    )
    block = unpack_square(total[0:8])[:, :RANK]
    coimage_ref[...] = lax.dot_general(
        block, inverse, (((0,), (1,)), ((), ())), precision=HIGHEST, preferred_element_type=F32
    )


def on_device(transport, test_panel):
    rows, cols = transport.shape
    total_rows = rows * lax.axis_size(("y", "z", "core"))
    ny, nz, nx = (lax.axis_size(name) for name in ("y", "z", "x"))
    chips = ny * nz
    flops = 2 * rows * cols * 128
    shape = jax.ShapeDtypeStruct

    halves = [test_panel[:16], test_panel[16:]]
    tile = jnp.concatenate(halves + halves, axis=1)
    other = lax.ppermute(tile, "core", [(0, 1), (1, 0)])
    mine = (lanes_of((16, 128)) < 64) == (lax.axis_index("core") == 0)
    pair = jnp.where(mine, tile, other)
    tiles = lax.all_to_all(jnp.broadcast_to(pair, (chips, 16, 128)), CHIPS, 0, 0)
    partial = kernel_call(
        first_sketch, shape((nx, RANK, rows), F32), flops, 5 << 20, tiles, transport
    )
    parts = lax.all_to_all(partial, "x", 0, 0)

    width = cols // (2 * nz)
    height = RANK * width // 128 + 8
    sums = kernel_call(
        middle_product, shape((2, nz, height, 128), F32), flops, 5 << 20, parts, transport
    )
    sums = jnp.sum(lax.all_to_all(sums, "core", 0, 0), axis=0)
    sums = jnp.sum(lax.all_to_all(sums, "z", 0, 0), axis=0)
    sums = lax.all_to_all(jnp.broadcast_to(sums, (ny, height, 128)), "y", 0, 0)
    panel = kernel_call(
        functools.partial(normalise, total_rows), shape((nz, RANK, width), BF16), 1 << 20, 1 << 20, sums
    )
    panel = lax.all_to_all(panel, "z", 0, 0)
    panel = lax.all_to_all(jnp.broadcast_to(panel, (2, nz, RANK, width)), "core", 0, 0)
    partial = kernel_call(
        next_sketch,
        shape((nx, RANK, rows), F32),
        flops,
        5 << 20,
        panel.reshape(2 * nz, RANK, width),
        transport,
    )
    parts = lax.all_to_all(partial, "x", 0, 0)

    sums, sketch = kernel_call(
        last_product,
        (shape((2, chips, 16, 128), F32), shape((RANK, rows), F32)),
        flops,
        6 << 20,
        parts,
        transport,
    )
    sums = jnp.sum(lax.all_to_all(sums, "core", 0, 0), axis=0)
    sums = lax.all_to_all(sums, CHIPS, 0, 0)
    basis, coimage = kernel_call(
        functools.partial(finish, total_rows),
        (shape((RANK, rows), F32), shape((RANK, RANK), F32)),
        1 << 20,
        1 << 20,
        sums,
        sketch,
    )
    return (basis.T, coimage)


def solution(mesh):
    sizes = {"cam": (("y", 8), ("z", 8), ("core", 2)), "proj": (("x", 4),)}
    names = [name for axis in mesh.axis_names for name, _ in sizes[axis]]
    shape = [size for axis in mesh.axis_names for _, size in sizes[axis]]
    fine = Mesh(np.asarray(mesh.devices).reshape(shape), names)
    rows = ("y", "z", "core")
    return jax.shard_map(
        on_device,
        mesh=fine,
        in_specs=(P(rows, "x"), P(("x",) + rows, None)),
        out_specs=(P(rows, None), P(("x",) + rows, None)),
        check_vma=False,
    )
```

```python
import functools

import jax
import jax.numpy as jnp
import numpy as np
from jax import lax
from jax.experimental import pallas as pl
from jax.experimental.pallas import tpu as pltpu
from jax.sharding import Mesh
from jax.sharding import PartitionSpec as P

CHIPS = ("y", "z")
RANK = 32
HIGHEST = lax.Precision.HIGHEST
F32 = jnp.float32
BF16 = jnp.bfloat16
VMEM = pl.BlockSpec(memory_space=pltpu.VMEM)
NT = (((1,), (1,)), ((), ()))
TN = (((0,), (0,)), ((), ()))


def kernel_call(body, outs, flops, moved, *args, streamed=None):
    specs, scratch = [VMEM] * len(args), []
    if streamed:
        specs[-1] = pl.BlockSpec(memory_space=pltpu.HBM)
        rows, cols = args[-1].shape
        scratch = [
            pltpu.VMEM((streamed, rows, cols // streamed), args[-1].dtype),
            pltpu.SemaphoreType.DMA((streamed,)),
        ]
    return pl.pallas_call(
        body,
        out_shape=outs,
        in_specs=specs,
        out_specs=jax.tree.map(lambda _: VMEM, outs),
        scratch_shapes=scratch,
        compiler_params=pltpu.CompilerParams(vmem_limit_bytes=(51 if streamed else 24) << 20),
        cost_estimate=pl.CostEstimate(flops=flops, bytes_accessed=moved, transcendentals=0),
    )(*args)


def lanes_of(shape):
    return lax.broadcasted_iota(jnp.int32, shape, len(shape) - 1)


def pack_square(square):
    lane = lanes_of((8, 128))
    out = jnp.where(lane < 32, square[0:8], 0.0)
    for q in range(1, 4):
        block = pltpu.roll(square[8 * q : 8 * q + 8], 32 * q, axis=1)
        out = jnp.where((lane >= 32 * q) & (lane < 32 * q + 32), block, out)
    return out


def unpack_square(tile):
    return jnp.concatenate([tile] + [pltpu.roll(tile, 128 - 32 * q, axis=1) for q in range(1, 4)])


def inverse_factor(gram):
    lane = lanes_of((RANK, 128))
    row = lax.broadcasted_iota(jnp.int32, (RANK, 128), 0)
    work = jnp.where(lane < RANK, gram, jnp.where(lane == row + RANK, 1.0, 0.0))
    pivots = jnp.ones((RANK, 128), F32)
    width = 8
    for start in range(0, RANK, width):
        columns = [
            jnp.broadcast_to(work[:, start + i : start + i + 1], (RANK, 128)) for i in range(width)
        ]
        for i in range(width):
            k = start + i
            pivot = jnp.broadcast_to(columns[i][k : k + 1], (RANK, 128))
            pivots = jnp.where(row == k, pivot, pivots)
            factor = jnp.where(row > k, columns[i] / pivot, 0.0)
            for later in range(i + 1, width):
                columns[later] = columns[later] - factor * columns[later][k : k + 1]
            work = work - factor * work[k : k + 1]
    return (work / jnp.sqrt(pivots))[:, RANK : 2 * RANK]


def stream(source_ref, blocks_ref, semaphores):
    width = blocks_ref.shape[2]
    copies = [
        pltpu.make_async_copy(
            source_ref.at[:, i * width : (i + 1) * width], blocks_ref.at[i], semaphores.at[i]
        )
        for i in range(blocks_ref.shape[0])
    ]
    for copy in copies:
        copy.start()

    def block(i):
        copies[i].wait()
        return blocks_ref[i]

    return block


def first_sketch(tiles_ref, transport_ref, out_ref, blocks_ref, semaphores):
    block = stream(transport_ref, blocks_ref, semaphores)
    chips, blocks = tiles_ref.shape[0], blocks_ref.shape[0]
    lane = lanes_of((16, 128))
    masks = [(lane >= 32 * q) & (lane < 32 * q + 32) for q in range(4)]
    total = jnp.zeros((transport_ref.shape[0], 128), F32)
    group = chips // blocks
    for i in range(blocks):
        rows = []
        for chip in range(i * group, (i + 1) * group):
            tile = tiles_ref[chip]
            rows += [jnp.where(mask, tile, jnp.zeros_like(tile)) for mask in masks]
        total += jnp.dot(block(i), jnp.concatenate(rows), preferred_element_type=F32)
    turned = total.T
    sketch = (turned[0:32] + turned[32:64]) + (turned[64:96] + turned[96:128])
    for copy in range(out_ref.shape[0]):
        out_ref[copy] = sketch


def next_sketch(panel_ref, transport_ref, out_ref, blocks_ref, semaphores):
    block = stream(transport_ref, blocks_ref, semaphores)
    groups, blocks = panel_ref.shape[0], blocks_ref.shape[0]
    each = groups // blocks
    sketch = jnp.zeros((RANK, transport_ref.shape[0]), F32)
    for i in range(blocks):
        panel = jnp.concatenate([panel_ref[i * each + g] for g in range(each)], axis=1)
        sketch += lax.dot_general(panel, block(i), NT, preferred_element_type=F32)
    for copy in range(out_ref.shape[0]):
        out_ref[copy] = sketch


def product(parts_ref, transport_ref, blocks_ref, semaphores):
    block = stream(transport_ref, blocks_ref, semaphores)
    sketch = (parts_ref[0] + parts_ref[1]) + (parts_ref[2] + parts_ref[3])
    gram = lax.dot_general(sketch, sketch, NT, precision=HIGHEST, preferred_element_type=F32)
    gram = jnp.concatenate([gram, jnp.zeros((RANK, 128 - RANK), F32)], axis=1)
    high = sketch.astype(BF16)
    low = (sketch - high.astype(F32)).astype(BF16)
    both = jnp.concatenate([high, low])

    def columns(i):
        out = jnp.dot(both, block(i), preferred_element_type=F32)
        return out[:RANK] + out[RANK:]

    return sketch, pack_square(gram), columns


def middle_product(parts_ref, transport_ref, out_ref, blocks_ref, semaphores):
    cores, groups, height, _ = out_ref.shape
    tiles = height // 8 - 1
    each = blocks_ref.shape[2] // 128 * 4 // tiles
    _, gram, columns = product(parts_ref, transport_ref, blocks_ref, semaphores)
    for core in range(cores):
        for wide in range(groups // each):
            block = columns(core * (groups // each) + wide)
            for g in range(each):
                for t in range(tiles):
                    a, c = t % 4, t // 4 + g * (tiles // 4)
                    out_ref[core, wide * each + g, 8 * t : 8 * t + 8] = block[
                        8 * a : 8 * a + 8, 128 * c : 128 * c + 128
                    ]
        for g in range(groups):
            out_ref[core, g, 8 * tiles : height] = gram


def last_product(parts_ref, transport_ref, out_ref, sketch_ref, blocks_ref, semaphores):
    cores, chips, _, _ = out_ref.shape
    sketch, gram, columns = product(parts_ref, transport_ref, blocks_ref, semaphores)
    sketch_ref[...] = sketch
    lane = lanes_of((8, 128))
    low_half, even = lane < 64, lane % 64 < 32
    for wide in range(chips // 8):
        block = columns(wide)
        for c in range(4):
            t = [block[8 * a : 8 * a + 8, 128 * c : 128 * c + 128] for a in range(4)]
            u = [None] * 4
            for a in (0, 1):
                u[a] = jnp.where(low_half, t[a], pltpu.roll(t[a + 2], 64, axis=1))
                u[a + 2] = jnp.where(low_half, pltpu.roll(t[a], 64, axis=1), t[a + 2])
            for a in (0, 2):
                v0 = jnp.where(even, u[a], pltpu.roll(u[a + 1], 32, axis=1))
                v1 = jnp.where(even, pltpu.roll(u[a], 96, axis=1), u[a + 1])
                for b, v in ((a, v0), (a + 1, v1)):
                    device = 16 * wide + 4 * c + b
                    out_ref[device % 2, device // 2, 0:8] = v
    for core in range(cores):
        for chip in range(chips):
            out_ref[core, chip, 8:16] = gram


def normalise(total_rows, sums_ref, out_ref):
    peers, height, _ = sums_ref.shape
    total = sums_ref[0]
    for p in range(1, peers):
        total = total + sums_ref[p]
    tiles = height // 8 - 1
    inverse = inverse_factor(unpack_square(total[8 * tiles :]) / total_rows)
    for c in range(tiles // 4):
        block = total[32 * c : 32 * c + 32]
        panel = jnp.dot(inverse, block, precision=HIGHEST, preferred_element_type=F32).astype(BF16)
        for copy in range(out_ref.shape[0]):
            out_ref[copy, :, 128 * c : 128 * c + 128] = panel


def finish(total_rows, sums_ref, sketch_ref, basis_ref, coimage_ref):
    total = sums_ref[0]
    for p in range(1, sums_ref.shape[0]):
        total = total + sums_ref[p]
    inverse = inverse_factor(unpack_square(total[8:16]) / total_rows)
    basis_ref[...] = jnp.dot(
        inverse, sketch_ref[...], precision=HIGHEST, preferred_element_type=F32
    )
    block = unpack_square(total[0:8])[:, :RANK]
    coimage_ref[...] = lax.dot_general(
        block, inverse, (((0,), (1,)), ((), ())), precision=HIGHEST, preferred_element_type=F32
    )


def on_device(transport, test_panel):
    rows, cols = transport.shape
    total_rows = rows * lax.axis_size(("y", "z", "core"))
    ny, nz, nx = (lax.axis_size(name) for name in ("y", "z", "x"))
    chips = ny * nz
    flops = 2 * rows * cols * 128
    shape = jax.ShapeDtypeStruct

    halves = [test_panel[:16], test_panel[16:]]
    tile = jnp.concatenate(halves + halves, axis=1)
    other = lax.ppermute(tile, "core", [(0, 1), (1, 0)])
    mine = (lanes_of((16, 128)) < 64) == (lax.axis_index("core") == 0)
    pair = jnp.where(mine, tile, other)
    tiles = lax.all_to_all(jnp.broadcast_to(pair, (chips, 16, 128)), CHIPS, 0, 0)
    partial = kernel_call(
        first_sketch, shape((nx, RANK, rows), F32), flops, 5 << 20, tiles, transport, streamed=8
    )
    parts = lax.all_to_all(partial, "x", 0, 0)

    width = cols // (2 * nz)
    height = RANK * width // 128 + 8
    sums = kernel_call(
        middle_product,
        shape((2, nz, height, 128), F32),
        flops,
        5 << 20,
        parts,
        transport,
        streamed=8,
    )
    sums = jnp.sum(lax.all_to_all(sums, "core", 0, 0), axis=0)
    sums = jnp.sum(lax.all_to_all(sums, "z", 0, 0), axis=0)
    sums = lax.all_to_all(jnp.broadcast_to(sums, (ny, height, 128)), "y", 0, 0)
    panel = kernel_call(
        functools.partial(normalise, total_rows), shape((nz, RANK, width), BF16), 1 << 20, 1 << 20, sums
    )
    panel = lax.all_to_all(panel, "z", 0, 0)
    panel = lax.all_to_all(jnp.broadcast_to(panel, (2, nz, RANK, width)), "core", 0, 0)
    partial = kernel_call(
        next_sketch,
        shape((nx, RANK, rows), F32),
        flops,
        5 << 20,
        panel.reshape(2 * nz, RANK, width),
        transport,
        streamed=8,
    )
    parts = lax.all_to_all(partial, "x", 0, 0)

    sums, sketch = kernel_call(
        last_product,
        (shape((2, chips, 16, 128), F32), shape((RANK, rows), F32)),
        flops,
        6 << 20,
        parts,
        transport,
        streamed=8,
    )
    sums = jnp.sum(lax.all_to_all(sums, "core", 0, 0), axis=0)
    sums = lax.all_to_all(sums, CHIPS, 0, 0)
    basis, coimage = kernel_call(
        functools.partial(finish, total_rows),
        (shape((RANK, rows), F32), shape((RANK, RANK), F32)),
        1 << 20,
        1 << 20,
        sums,
        sketch,
    )
    return (basis.T, coimage)


def solution(mesh):
    sizes = {"cam": (("y", 8), ("z", 8), ("core", 2)), "proj": (("x", 4),)}
    names = [name for axis in mesh.axis_names for name, _ in sizes[axis]]
    shape = [size for axis in mesh.axis_names for _, size in sizes[axis]]
    fine = Mesh(np.asarray(mesh.devices).reshape(shape), names)
    rows = ("y", "z", "core")
    return jax.shard_map(
        on_device,
        mesh=fine,
        in_specs=(P(rows, "x"), P(("x",) + rows, None)),
        out_specs=(P(rows, None), P(("x",) + rows, None)),
        check_vma=False,
    )
```

```python
import functools

import jax
import jax.numpy as jnp
import numpy as np
from jax import lax
from jax.experimental import pallas as pl
from jax.experimental.pallas import tpu as pltpu
from jax.sharding import Mesh
from jax.sharding import PartitionSpec as P

CHIPS = ("y", "z")
RANK = 32
HIGHEST = lax.Precision.HIGHEST
F32 = jnp.float32
BF16 = jnp.bfloat16
VMEM = pl.BlockSpec(memory_space=pltpu.VMEM)
NT = (((1,), (1,)), ((), ()))
TN = (((0,), (0,)), ((), ()))


def kernel_call(body, outs, flops, moved, *args):
    return pl.pallas_call(
        body,
        out_shape=outs,
        in_specs=[VMEM] * len(args),
        out_specs=jax.tree.map(lambda _: VMEM, outs),
        compiler_params=pltpu.CompilerParams(vmem_limit_bytes=24 << 20),
        cost_estimate=pl.CostEstimate(flops=flops, bytes_accessed=moved, transcendentals=0),
    )(*args)


def lanes_of(shape):
    return lax.broadcasted_iota(jnp.int32, shape, len(shape) - 1)


def pack_square(square):
    lane = lanes_of((8, 128))
    out = jnp.where(lane < 32, square[0:8], 0.0)
    for q in range(1, 4):
        block = pltpu.roll(square[8 * q : 8 * q + 8], 32 * q, axis=1)
        out = jnp.where((lane >= 32 * q) & (lane < 32 * q + 32), block, out)
    return out


def unpack_square(tile):
    return jnp.concatenate([tile] + [pltpu.roll(tile, 128 - 32 * q, axis=1) for q in range(1, 4)])


def inverse_factor(gram):
    lane = lanes_of((RANK, 128))
    row = lax.broadcasted_iota(jnp.int32, (RANK, 128), 0)
    work = jnp.where(lane < RANK, gram, jnp.where(lane == row + RANK, 1.0, 0.0))
    pivots = jnp.ones((RANK, 128), F32)
    width = 8
    for start in range(0, RANK, width):
        columns = [
            jnp.broadcast_to(work[:, start + i : start + i + 1], (RANK, 128)) for i in range(width)
        ]
        for i in range(width):
            k = start + i
            pivot = jnp.broadcast_to(columns[i][k : k + 1], (RANK, 128))
            pivots = jnp.where(row == k, pivot, pivots)
            factor = jnp.where(row > k, columns[i] / pivot, 0.0)
            for later in range(i + 1, width):
                columns[later] = columns[later] - factor * columns[later][k : k + 1]
            work = work - factor * work[k : k + 1]
    return (work / jnp.sqrt(pivots))[:, RANK : 2 * RANK]


def fan_out(pair_ref, out_ref):
    for copy in range(out_ref.shape[0]):
        out_ref[copy] = pair_ref[...]


def first_sketch(tiles_ref, transport_ref, out_ref):
    chips, cols = tiles_ref.shape[0], transport_ref.shape[1]
    lane = lanes_of((16, 128))
    masks = [(lane >= 32 * q) & (lane < 32 * q + 32) for q in range(4)]
    total = jnp.zeros((transport_ref.shape[0], 128), F32)
    group = 8
    for start in range(0, chips, group):
        rows = []
        for chip in range(start, start + group):
            tile = tiles_ref[chip]
            rows += [jnp.where(mask, tile, jnp.zeros_like(tile)) for mask in masks]
        at = start * (cols // chips)
        total += jnp.dot(
            transport_ref[:, at : at + group * (cols // chips)],
            jnp.concatenate(rows),
            preferred_element_type=F32,
        )
    turned = total.T
    sketch = (turned[0:32] + turned[32:64]) + (turned[64:96] + turned[96:128])
    for copy in range(out_ref.shape[0]):
        out_ref[copy] = sketch


def next_sketch(panel_ref, transport_ref, out_ref):
    groups, _, width = panel_ref.shape
    sketch = jnp.zeros((RANK, transport_ref.shape[0]), F32)
    for g in range(groups):
        sketch += lax.dot_general(
            panel_ref[g],
            transport_ref[:, g * width : (g + 1) * width],
            NT,
            preferred_element_type=F32,
        )
    for copy in range(out_ref.shape[0]):
        out_ref[copy] = sketch


def product(parts_ref, transport_ref):
    sketch = (parts_ref[0] + parts_ref[1]) + (parts_ref[2] + parts_ref[3])
    gram = lax.dot_general(sketch, sketch, NT, precision=HIGHEST, preferred_element_type=F32)
    gram = jnp.concatenate([gram, jnp.zeros((RANK, 128 - RANK), F32)], axis=1)
    high = sketch.astype(BF16)
    low = (sketch - high.astype(F32)).astype(BF16)
    both = jnp.concatenate([high, low])

    def columns(at, width):
        out = jnp.dot(both, transport_ref[:, at : at + width], preferred_element_type=F32)
        return out[:RANK] + out[RANK:]

    return sketch, pack_square(gram), columns


def middle_product(parts_ref, transport_ref, out_ref):
    cores, groups, height, _ = out_ref.shape
    tiles = height // 8 - 1
    width = tiles // 4 * 128
    _, gram, columns = product(parts_ref, transport_ref)
    for core in range(cores):
        for g in range(groups):
            block = columns((core * groups + g) * width, width)
            for t in range(tiles):
                a, c = t % 4, t // 4
                out_ref[core, g, 8 * t : 8 * t + 8] = block[8 * a : 8 * a + 8, 128 * c : 128 * c + 128]
            out_ref[core, g, 8 * tiles : height] = gram


def last_product(parts_ref, transport_ref, out_ref, sketch_ref):
    cores, chips, _, _ = out_ref.shape
    sketch, gram, columns = product(parts_ref, transport_ref)
    sketch_ref[...] = sketch
    lane = lanes_of((8, 128))
    low_half, even = lane < 64, lane % 64 < 32
    for wide in range(chips // 8):
        block = columns(512 * wide, 512)
        for c in range(4):
            t = [block[8 * a : 8 * a + 8, 128 * c : 128 * c + 128] for a in range(4)]
            u = [None] * 4
            for a in (0, 1):
                u[a] = jnp.where(low_half, t[a], pltpu.roll(t[a + 2], 64, axis=1))
                u[a + 2] = jnp.where(low_half, pltpu.roll(t[a], 64, axis=1), t[a + 2])
            for a in (0, 2):
                v0 = jnp.where(even, u[a], pltpu.roll(u[a + 1], 32, axis=1))
                v1 = jnp.where(even, pltpu.roll(u[a], 96, axis=1), u[a + 1])
                for b, v in ((a, v0), (a + 1, v1)):
                    device = 16 * wide + 4 * c + b
                    out_ref[device % 2, device // 2, 0:8] = v
    for core in range(cores):
        for chip in range(chips):
            out_ref[core, chip, 8:16] = gram


def normalise(total_rows, sums_ref, out_ref):
    peers, height, _ = sums_ref.shape
    total = sums_ref[0]
    for p in range(1, peers):
        total = total + sums_ref[p]
    tiles = height // 8 - 1
    inverse = inverse_factor(unpack_square(total[8 * tiles :]) / total_rows)
    for c in range(tiles // 4):
        block = total[32 * c : 32 * c + 32]
        panel = jnp.dot(inverse, block, precision=HIGHEST, preferred_element_type=F32).astype(BF16)
        for copy in range(out_ref.shape[0]):
            out_ref[copy, :, 128 * c : 128 * c + 128] = panel


def finish(total_rows, sums_ref, sketch_ref, basis_ref, coimage_ref):
    total = sums_ref[0]
    for p in range(1, sums_ref.shape[0]):
        total = total + sums_ref[p]
    inverse = inverse_factor(unpack_square(total[8:16]) / total_rows)
    basis_ref[...] = jnp.dot(
        inverse, sketch_ref[...], precision=HIGHEST, preferred_element_type=F32
    )
    block = unpack_square(total[0:8])[:, :RANK]
    coimage_ref[...] = lax.dot_general(
        block, inverse, (((0,), (1,)), ((), ())), precision=HIGHEST, preferred_element_type=F32
    )


def on_device(transport, test_panel):
    rows, cols = transport.shape
    total_rows = rows * lax.axis_size(("y", "z", "core"))
    ny, nz, nx = (lax.axis_size(name) for name in ("y", "z", "x"))
    chips = ny * nz
    flops = 2 * rows * cols * 128
    shape = jax.ShapeDtypeStruct

    halves = [test_panel[:16], test_panel[16:]]
    tile = jnp.concatenate(halves + halves, axis=1)
    other = lax.ppermute(tile, "core", [(0, 1), (1, 0)])
    mine = (lanes_of((16, 128)) < 64) == (lax.axis_index("core") == 0)
    pair = jnp.where(mine, tile, other)
    copies = kernel_call(fan_out, shape((chips, 16, 128), BF16), 1 << 32, 8 << 20, pair)
    tiles = lax.all_to_all(copies, CHIPS, 0, 0)
    partial = kernel_call(
        first_sketch, shape((nx, RANK, rows), F32), flops, 5 << 20, tiles, transport
    )
    parts = lax.all_to_all(partial, "x", 0, 0)

    width = cols // (2 * nz)
    height = RANK * width // 128 + 8
    sums = kernel_call(
        middle_product, shape((2, nz, height, 128), F32), flops, 5 << 20, parts, transport
    )
    sums = jnp.sum(lax.all_to_all(sums, "core", 0, 0), axis=0)
    sums = jnp.sum(lax.all_to_all(sums, "z", 0, 0), axis=0)
    sums = lax.all_to_all(jnp.broadcast_to(sums, (ny, height, 128)), "y", 0, 0)
    panel = kernel_call(
        functools.partial(normalise, total_rows), shape((nz, RANK, width), BF16), 1 << 32, 8 << 20, sums
    )
    panel = lax.all_to_all(panel, "z", 0, 0)
    panel = lax.all_to_all(jnp.broadcast_to(panel, (2, nz, RANK, width)), "core", 0, 0)
    partial = kernel_call(
        next_sketch,
        shape((nx, RANK, rows), F32),
        flops,
        5 << 20,
        panel.reshape(2 * nz, RANK, width),
        transport,
    )
    parts = lax.all_to_all(partial, "x", 0, 0)

    sums, sketch = kernel_call(
        last_product,
        (shape((2, chips, 16, 128), F32), shape((RANK, rows), F32)),
        flops,
        6 << 20,
        parts,
        transport,
    )
    sums = jnp.sum(lax.all_to_all(sums, "core", 0, 0), axis=0)
    sums = lax.all_to_all(sums, CHIPS, 0, 0)
    basis, coimage = kernel_call(
        functools.partial(finish, total_rows),
        (shape((RANK, rows), F32), shape((RANK, RANK), F32)),
        1 << 20,
        1 << 20,
        sums,
        sketch,
    )
    return (basis.T, coimage)


def solution(mesh):
    sizes = {"cam": (("y", 8), ("z", 8), ("core", 2)), "proj": (("x", 4),)}
    names = [name for axis in mesh.axis_names for name, _ in sizes[axis]]
    shape = [size for axis in mesh.axis_names for _, size in sizes[axis]]
    fine = Mesh(np.asarray(mesh.devices).reshape(shape), names)
    rows = ("y", "z", "core")
    return jax.shard_map(
        on_device,
        mesh=fine,
        in_specs=(P(rows, "x"), P(("x",) + rows, None)),
        out_specs=(P(rows, None), P(("x",) + rows, None)),
        check_vma=False,
    )
```

```python
import functools

import jax
import jax.numpy as jnp
import numpy as np
from jax import lax
from jax.experimental import pallas as pl
from jax.experimental.pallas import tpu as pltpu
from jax.sharding import Mesh
from jax.sharding import PartitionSpec as P

CHIPS = ("y", "z")
RANK = 32
HIGHEST = lax.Precision.HIGHEST
F32 = jnp.float32
BF16 = jnp.bfloat16
VMEM = pl.BlockSpec(memory_space=pltpu.VMEM)
NT = (((1,), (1,)), ((), ()))
TN = (((0,), (0,)), ((), ()))


def kernel_call(body, outs, flops, moved, *args):
    return pl.pallas_call(
        body,
        out_shape=outs,
        in_specs=[VMEM] * len(args),
        out_specs=jax.tree.map(lambda _: VMEM, outs),
        compiler_params=pltpu.CompilerParams(vmem_limit_bytes=24 << 20),
        cost_estimate=pl.CostEstimate(flops=flops, bytes_accessed=moved, transcendentals=0),
    )(*args)


def lanes_of(shape):
    return lax.broadcasted_iota(jnp.int32, shape, len(shape) - 1)


def pack_square(square):
    lane = lanes_of((8, 128))
    out = jnp.where(lane < 32, square[0:8], 0.0)
    for q in range(1, 4):
        block = pltpu.roll(square[8 * q : 8 * q + 8], 32 * q, axis=1)
        out = jnp.where((lane >= 32 * q) & (lane < 32 * q + 32), block, out)
    return out


def unpack_square(tile):
    return jnp.concatenate([tile] + [pltpu.roll(tile, 128 - 32 * q, axis=1) for q in range(1, 4)])


def inverse_factor(gram):
    lane = lanes_of((RANK, 128))
    row = lax.broadcasted_iota(jnp.int32, (RANK, 128), 0)
    work = jnp.where(lane < RANK, gram, jnp.where(lane == row + RANK, 1.0, 0.0))
    pivots = jnp.ones((RANK, 128), F32)
    width = 8
    for start in range(0, RANK, width):
        columns = [
            jnp.broadcast_to(work[:, start + i : start + i + 1], (RANK, 128)) for i in range(width)
        ]
        for i in range(width):
            k = start + i
            pivot = jnp.broadcast_to(columns[i][k : k + 1], (RANK, 128))
            pivots = jnp.where(row == k, pivot, pivots)
            factor = jnp.where(row > k, columns[i] / pivot, 0.0)
            for later in range(i + 1, width):
                columns[later] = columns[later] - factor * columns[later][k : k + 1]
            work = work - factor * work[k : k + 1]
    return (work / jnp.sqrt(pivots))[:, RANK : 2 * RANK]


def fan_out(panel_ref, out_ref):
    panel = jnp.concatenate([panel_ref[...].astype(F32), jnp.zeros((RANK, 128 - RANK), F32)], axis=1)
    tile = pack_square(panel).astype(BF16)
    for copy in range(out_ref.shape[0]):
        out_ref[copy] = tile


def first_sketch(tiles_ref, transport_ref, out_ref):
    cores, chips = tiles_ref.shape[:2]
    cols = transport_ref.shape[1]
    lane = lanes_of((8, 128))
    masks = [(lane >= 32 * q) & (lane < 32 * q + 32) for q in range(4)]
    total = jnp.zeros((transport_ref.shape[0], 128), F32)
    group = 8
    for start in range(0, chips, group):
        rows = []
        for chip in range(start, start + group):
            for core in range(cores):
                tile = tiles_ref[core, chip].astype(F32)
                rows += [jnp.where(mask, tile, 0.0) for mask in masks]
        at = start * (cols // chips)
        total += jnp.dot(
            transport_ref[:, at : at + group * (cols // chips)],
            jnp.concatenate(rows).astype(BF16),
            preferred_element_type=F32,
        )
    turned = total.T
    sketch = (turned[0:32] + turned[32:64]) + (turned[64:96] + turned[96:128])
    for copy in range(out_ref.shape[0]):
        out_ref[copy] = sketch


def next_sketch(panel_ref, transport_ref, out_ref):
    groups, _, width = panel_ref.shape
    sketch = jnp.zeros((RANK, transport_ref.shape[0]), F32)
    for g in range(groups):
        sketch += lax.dot_general(
            panel_ref[g],
            transport_ref[:, g * width : (g + 1) * width],
            NT,
            preferred_element_type=F32,
        )
    for copy in range(out_ref.shape[0]):
        out_ref[copy] = sketch


def product(parts_ref, transport_ref):
    sketch = (parts_ref[0] + parts_ref[1]) + (parts_ref[2] + parts_ref[3])
    gram = lax.dot_general(sketch, sketch, NT, precision=HIGHEST, preferred_element_type=F32)
    gram = jnp.concatenate([gram, jnp.zeros((RANK, 128 - RANK), F32)], axis=1)
    high = sketch.astype(BF16)
    low = (sketch - high.astype(F32)).astype(BF16)
    both = jnp.concatenate([high, low])

    def columns(at, width):
        out = jnp.dot(both, transport_ref[:, at : at + width], preferred_element_type=F32)
        return out[:RANK] + out[RANK:]

    return sketch, pack_square(gram), columns


def middle_product(parts_ref, transport_ref, out_ref):
    cores, groups, height, _ = out_ref.shape
    tiles = height // 8 - 1
    width = tiles // 4 * 128
    _, gram, columns = product(parts_ref, transport_ref)
    for core in range(cores):
        for g in range(groups):
            block = columns((core * groups + g) * width, width)
            for t in range(tiles):
                a, c = t % 4, t // 4
                out_ref[core, g, 8 * t : 8 * t + 8] = block[8 * a : 8 * a + 8, 128 * c : 128 * c + 128]
            out_ref[core, g, 8 * tiles : height] = gram


def last_product(parts_ref, transport_ref, out_ref, sketch_ref):
    cores, chips, _, _ = out_ref.shape
    sketch, gram, columns = product(parts_ref, transport_ref)
    sketch_ref[...] = sketch
    lane = lanes_of((8, 128))
    low_half, even = lane < 64, lane % 64 < 32
    for wide in range(chips // 8):
        block = columns(512 * wide, 512)
        for c in range(4):
            t = [block[8 * a : 8 * a + 8, 128 * c : 128 * c + 128] for a in range(4)]
            u = [None] * 4
            for a in (0, 1):
                u[a] = jnp.where(low_half, t[a], pltpu.roll(t[a + 2], 64, axis=1))
                u[a + 2] = jnp.where(low_half, pltpu.roll(t[a], 64, axis=1), t[a + 2])
            for a in (0, 2):
                v0 = jnp.where(even, u[a], pltpu.roll(u[a + 1], 32, axis=1))
                v1 = jnp.where(even, pltpu.roll(u[a], 96, axis=1), u[a + 1])
                for b, v in ((a, v0), (a + 1, v1)):
                    device = 16 * wide + 4 * c + b
                    out_ref[device % 2, device // 2, 0:8] = v
    for core in range(cores):
        for chip in range(chips):
            out_ref[core, chip, 8:16] = gram


def normalise(total_rows, sums_ref, out_ref):
    peers, height, _ = sums_ref.shape
    total = sums_ref[0]
    for p in range(1, peers):
        total = total + sums_ref[p]
    tiles = height // 8 - 1
    inverse = inverse_factor(unpack_square(total[8 * tiles :]) / total_rows)
    for c in range(tiles // 4):
        block = total[32 * c : 32 * c + 32]
        panel = jnp.dot(inverse, block, precision=HIGHEST, preferred_element_type=F32).astype(BF16)
        for copy in range(out_ref.shape[0]):
            out_ref[copy, :, 128 * c : 128 * c + 128] = panel


def finish(total_rows, sums_ref, sketch_ref, basis_ref, coimage_ref):
    total = sums_ref[0]
    for p in range(1, sums_ref.shape[0]):
        total = total + sums_ref[p]
    inverse = inverse_factor(unpack_square(total[8:16]) / total_rows)
    basis_ref[...] = jnp.dot(
        inverse, sketch_ref[...], precision=HIGHEST, preferred_element_type=F32
    )
    block = unpack_square(total[0:8])[:, :RANK]
    coimage_ref[...] = lax.dot_general(
        block, inverse, (((0,), (1,)), ((), ())), precision=HIGHEST, preferred_element_type=F32
    )


def on_device(transport, test_panel):
    rows, cols = transport.shape
    total_rows = rows * lax.axis_size(("y", "z", "core"))
    ny, nz, nx = (lax.axis_size(name) for name in ("y", "z", "x"))
    chips = ny * nz
    flops = 2 * rows * cols * 128
    shape = jax.ShapeDtypeStruct

    copies = kernel_call(fan_out, shape((chips, 8, 128), BF16), 1 << 32, 8 << 20, test_panel)
    tiles = lax.all_to_all(copies, CHIPS, 0, 0)
    tiles = lax.all_to_all(jnp.broadcast_to(tiles, (2, chips, 8, 128)), "core", 0, 0)
    partial = kernel_call(
        first_sketch, shape((nx, RANK, rows), F32), flops, 5 << 20, tiles, transport
    )
    parts = lax.all_to_all(partial, "x", 0, 0)

    width = cols // (2 * ny)
    height = RANK * width // 128 + 8
    sums = kernel_call(
        middle_product, shape((2, ny, height, 128), F32), flops, 5 << 20, parts, transport
    )
    sums = jnp.sum(lax.all_to_all(sums, "core", 0, 0), axis=0)
    sums = jnp.sum(lax.all_to_all(sums, "y", 0, 0), axis=0)
    sums = lax.all_to_all(jnp.broadcast_to(sums, (nz, height, 128)), "z", 0, 0)
    panel = kernel_call(
        functools.partial(normalise, total_rows),
        shape((2 * ny, RANK, width), BF16),
        1 << 32,
        8 << 20,
        sums,
    )
    panel = lax.all_to_all(panel, ("core", "y"), 0, 0)
    partial = kernel_call(
        next_sketch,
        shape((nx, RANK, rows), F32),
        flops,
        5 << 20,
        panel,
        transport,
    )
    parts = lax.all_to_all(partial, "x", 0, 0)

    sums, sketch = kernel_call(
        last_product,
        (shape((2, chips, 16, 128), F32), shape((RANK, rows), F32)),
        flops,
        6 << 20,
        parts,
        transport,
    )
    sums = jnp.sum(lax.all_to_all(sums, "core", 0, 0), axis=0)
    sums = lax.all_to_all(sums, CHIPS, 0, 0)
    basis, coimage = kernel_call(
        functools.partial(finish, total_rows),
        (shape((RANK, rows), F32), shape((RANK, RANK), F32)),
        1 << 20,
        1 << 20,
        sums,
        sketch,
    )
    return (basis.T, coimage)


def solution(mesh):
    sizes = {"cam": (("y", 8), ("z", 8), ("core", 2)), "proj": (("x", 4),)}
    names = [name for axis in mesh.axis_names for name, _ in sizes[axis]]
    shape = [size for axis in mesh.axis_names for _, size in sizes[axis]]
    fine = Mesh(np.asarray(mesh.devices).reshape(shape), names)
    rows = ("y", "z", "core")
    return jax.shard_map(
        on_device,
        mesh=fine,
        in_specs=(P(rows, "x"), P(("x",) + rows, None)),
        out_specs=(P(rows, None), P(("x",) + rows, None)),
        check_vma=False,
    )
```

```python
import functools

import jax
import jax.numpy as jnp
import numpy as np
from jax import lax
from jax.experimental import pallas as pl
from jax.experimental.pallas import tpu as pltpu
from jax.sharding import Mesh
from jax.sharding import PartitionSpec as P

CHIPS = ("y", "z")
RANK = 32
HIGHEST = lax.Precision.HIGHEST
F32 = jnp.float32
BF16 = jnp.bfloat16
VMEM = pl.BlockSpec(memory_space=pltpu.VMEM)
NT = (((1,), (1,)), ((), ()))
TN = (((0,), (0,)), ((), ()))


def kernel_call(body, outs, flops, moved, *args):
    return pl.pallas_call(
        body,
        out_shape=outs,
        in_specs=[VMEM] * len(args),
        out_specs=jax.tree.map(lambda _: VMEM, outs),
        compiler_params=pltpu.CompilerParams(vmem_limit_bytes=24 << 20),
        cost_estimate=pl.CostEstimate(flops=flops, bytes_accessed=moved, transcendentals=0),
    )(*args)


def lanes_of(shape):
    return lax.broadcasted_iota(jnp.int32, shape, len(shape) - 1)


def pack_square(square):
    lane = lanes_of((8, 128))
    out = jnp.where(lane < 32, square[0:8], 0.0)
    for q in range(1, 4):
        block = pltpu.roll(square[8 * q : 8 * q + 8], 32 * q, axis=1)
        out = jnp.where((lane >= 32 * q) & (lane < 32 * q + 32), block, out)
    return out


def unpack_square(tile):
    return jnp.concatenate([tile] + [pltpu.roll(tile, 128 - 32 * q, axis=1) for q in range(1, 4)])


def inverse_factor(gram):
    lane = lanes_of((RANK, 128))
    row = lax.broadcasted_iota(jnp.int32, (RANK, 128), 0)
    work = jnp.where(lane < RANK, gram, jnp.where(lane == row + RANK, 1.0, 0.0))
    pivots = jnp.ones((RANK, 128), F32)
    width = 8
    for start in range(0, RANK, width):
        columns = [
            jnp.broadcast_to(work[:, start + i : start + i + 1], (RANK, 128)) for i in range(width)
        ]
        for i in range(width):
            k = start + i
            pivot = jnp.broadcast_to(columns[i][k : k + 1], (RANK, 128))
            pivots = jnp.where(row == k, pivot, pivots)
            factor = jnp.where(row > k, columns[i] / pivot, 0.0)
            for later in range(i + 1, width):
                columns[later] = columns[later] - factor * columns[later][k : k + 1]
            work = work - factor * work[k : k + 1]
    return (work / jnp.sqrt(pivots))[:, RANK : 2 * RANK]


def fan_out(panel_ref, out_ref):
    panel = jnp.concatenate([panel_ref[...].astype(F32), jnp.zeros((RANK, 128 - RANK), F32)], axis=1)
    tile = pack_square(panel).astype(BF16)
    for copy in range(out_ref.shape[0]):
        out_ref[copy] = tile


def first_sketch(tiles_ref, transport_ref, out_ref):
    cores, chips = tiles_ref.shape[:2]
    cols = transport_ref.shape[1]
    lane = lanes_of((8, 128))
    masks = [(lane >= 32 * q) & (lane < 32 * q + 32) for q in range(4)]
    total = jnp.zeros((transport_ref.shape[0], 128), F32)
    group = 8
    for start in range(0, chips, group):
        rows = []
        for chip in range(start, start + group):
            for core in range(cores):
                tile = tiles_ref[core, chip].astype(F32)
                rows += [jnp.where(mask, tile, 0.0) for mask in masks]
        at = start * (cols // chips)
        total += jnp.dot(
            transport_ref[:, at : at + group * (cols // chips)],
            jnp.concatenate(rows).astype(BF16),
            preferred_element_type=F32,
        )
    turned = total.T
    sketch = (turned[0:32] + turned[32:64]) + (turned[64:96] + turned[96:128])
    for copy in range(out_ref.shape[0]):
        out_ref[copy] = sketch


def next_sketch(panel_ref, transport_ref, out_ref):
    groups, _, width = panel_ref.shape
    sketch = jnp.zeros((RANK, transport_ref.shape[0]), F32)
    for g in range(groups):
        sketch += lax.dot_general(
            panel_ref[g],
            transport_ref[:, g * width : (g + 1) * width],
            NT,
            preferred_element_type=F32,
        )
    for copy in range(out_ref.shape[0]):
        out_ref[copy] = sketch


def product(parts_ref, transport_ref):
    sketch = (parts_ref[0] + parts_ref[1]) + (parts_ref[2] + parts_ref[3])
    gram = lax.dot_general(sketch, sketch, NT, precision=HIGHEST, preferred_element_type=F32)
    gram = jnp.concatenate([gram, jnp.zeros((RANK, 128 - RANK), F32)], axis=1)
    high = sketch.astype(BF16)
    low = (sketch - high.astype(F32)).astype(BF16)
    both = jnp.concatenate([high, low])

    def columns(at, width):
        out = jnp.dot(both, transport_ref[:, at : at + width], preferred_element_type=F32)
        return out[:RANK] + out[RANK:]

    return sketch, pack_square(gram), columns


def middle_product(parts_ref, transport_ref, out_ref):
    cores, groups, height, _ = out_ref.shape
    tiles = height // 8 - 1
    width = tiles // 4 * 128
    _, gram, columns = product(parts_ref, transport_ref)
    for core in range(cores):
        for g in range(groups):
            block = columns((core * groups + g) * width, width)
            for t in range(tiles):
                a, c = t % 4, t // 4
                out_ref[core, g, 8 * t : 8 * t + 8] = block[8 * a : 8 * a + 8, 128 * c : 128 * c + 128]
            out_ref[core, g, 8 * tiles : height] = gram


def last_product(parts_ref, transport_ref, out_ref, sketch_ref):
    cores, chips, _, _ = out_ref.shape
    sketch, gram, columns = product(parts_ref, transport_ref)
    sketch_ref[...] = sketch
    lane = lanes_of((8, 128))
    low_half, even = lane < 64, lane % 64 < 32
    for wide in range(chips // 8):
        block = columns(512 * wide, 512)
        for c in range(4):
            t = [block[8 * a : 8 * a + 8, 128 * c : 128 * c + 128] for a in range(4)]
            u = [None] * 4
            for a in (0, 1):
                u[a] = jnp.where(low_half, t[a], pltpu.roll(t[a + 2], 64, axis=1))
                u[a + 2] = jnp.where(low_half, pltpu.roll(t[a], 64, axis=1), t[a + 2])
            for a in (0, 2):
                v0 = jnp.where(even, u[a], pltpu.roll(u[a + 1], 32, axis=1))
                v1 = jnp.where(even, pltpu.roll(u[a], 96, axis=1), u[a + 1])
                for b, v in ((a, v0), (a + 1, v1)):
                    device = 16 * wide + 4 * c + b
                    out_ref[device % 2, device // 2, 0:8] = v
    for core in range(cores):
        for chip in range(chips):
            out_ref[core, chip, 8:16] = gram


def encode(total):
    gram = total[-8:]
    terms = []
    for _ in range(3):
        terms.append(gram.astype(BF16).astype(F32))
        gram = gram - terms[-1]
    return jnp.concatenate([total[:-8]] + terms).astype(BF16)


def decoded_sum(messages_ref):
    total = messages_ref[0].astype(F32)
    for p in range(1, messages_ref.shape[0]):
        total = total + messages_ref[p].astype(F32)
    gram = (total[-8:] + total[-16:-8]) + total[-24:-16]
    return jnp.concatenate([total[:-24], gram])


def add_cores(sums_ref, out_ref):
    for peer in range(out_ref.shape[0]):
        out_ref[peer] = encode(sums_ref[0, peer] + sums_ref[1, peer])


def add_peers(messages_ref, out_ref):
    message = encode(decoded_sum(messages_ref))
    for copy in range(out_ref.shape[0]):
        out_ref[copy] = message


def normalise(total_rows, messages_ref, out_ref):
    total = decoded_sum(messages_ref)
    tiles = total.shape[0] // 8 - 1
    inverse = inverse_factor(unpack_square(total[8 * tiles :]) / total_rows)
    for c in range(tiles // 4):
        block = total[32 * c : 32 * c + 32]
        panel = jnp.dot(inverse, block, precision=HIGHEST, preferred_element_type=F32).astype(BF16)
        for copy in range(out_ref.shape[0]):
            out_ref[copy, :, 128 * c : 128 * c + 128] = panel


def finish(total_rows, sums_ref, sketch_ref, basis_ref, coimage_ref):
    total = sums_ref[0]
    for p in range(1, sums_ref.shape[0]):
        total = total + sums_ref[p]
    inverse = inverse_factor(unpack_square(total[8:16]) / total_rows)
    basis_ref[...] = jnp.dot(
        inverse, sketch_ref[...], precision=HIGHEST, preferred_element_type=F32
    )
    block = unpack_square(total[0:8])[:, :RANK]
    coimage_ref[...] = lax.dot_general(
        block, inverse, (((0,), (1,)), ((), ())), precision=HIGHEST, preferred_element_type=F32
    )


def on_device(transport, test_panel):
    rows, cols = transport.shape
    total_rows = rows * lax.axis_size(("y", "z", "core"))
    ny, nz, nx = (lax.axis_size(name) for name in ("y", "z", "x"))
    chips = ny * nz
    flops = 2 * rows * cols * 128
    shape = jax.ShapeDtypeStruct

    copies = kernel_call(fan_out, shape((chips, 8, 128), BF16), 1 << 32, 8 << 20, test_panel)
    tiles = lax.all_to_all(copies, CHIPS, 0, 0)
    tiles = lax.all_to_all(jnp.broadcast_to(tiles, (2, chips, 8, 128)), "core", 0, 0)
    partial = kernel_call(
        first_sketch, shape((nx, RANK, rows), F32), flops, 5 << 20, tiles, transport
    )
    parts = lax.all_to_all(partial, "x", 0, 0)

    width = cols // (2 * ny)
    height = RANK * width // 128 + 8
    sums = kernel_call(
        middle_product, shape((2, ny, height, 128), F32), flops, 5 << 20, parts, transport
    )
    sums = lax.all_to_all(sums, "core", 0, 0)
    sums = kernel_call(add_cores, shape((ny, height + 16, 128), BF16), 0, 1 << 20, sums)
    sums = lax.all_to_all(sums, "y", 0, 0)
    sums = kernel_call(add_peers, shape((nz, height + 16, 128), BF16), 0, 1 << 20, sums)
    sums = lax.all_to_all(sums, "z", 0, 0)
    panel = kernel_call(
        functools.partial(normalise, total_rows),
        shape((2 * ny, RANK, width), BF16),
        1 << 32,
        8 << 20,
        sums,
    )
    panel = lax.all_to_all(panel, ("core", "y"), 0, 0)
    partial = kernel_call(
        next_sketch,
        shape((nx, RANK, rows), F32),
        flops,
        5 << 20,
        panel,
        transport,
    )
    parts = lax.all_to_all(partial, "x", 0, 0)

    sums, sketch = kernel_call(
        last_product,
        (shape((2, chips, 16, 128), F32), shape((RANK, rows), F32)),
        flops,
        6 << 20,
        parts,
        transport,
    )
    sums = jnp.sum(lax.all_to_all(sums, "core", 0, 0), axis=0)
    sums = lax.all_to_all(sums, CHIPS, 0, 0)
    basis, coimage = kernel_call(
        functools.partial(finish, total_rows),
        (shape((RANK, rows), F32), shape((RANK, RANK), F32)),
        1 << 20,
        1 << 20,
        sums,
        sketch,
    )
    return (basis.T, coimage)


def solution(mesh):
    sizes = {"cam": (("y", 8), ("z", 8), ("core", 2)), "proj": (("x", 4),)}
    names = [name for axis in mesh.axis_names for name, _ in sizes[axis]]
    shape = [size for axis in mesh.axis_names for _, size in sizes[axis]]
    fine = Mesh(np.asarray(mesh.devices).reshape(shape), names)
    rows = ("y", "z", "core")
    return jax.shard_map(
        on_device,
        mesh=fine,
        in_specs=(P(rows, "x"), P(("x",) + rows, None)),
        out_specs=(P(rows, None), P(("x",) + rows, None)),
        check_vma=False,
    )
```

```python
import functools

import jax
import jax.numpy as jnp
import numpy as np
from jax import lax
from jax.experimental import pallas as pl
from jax.experimental.pallas import tpu as pltpu
from jax.sharding import Mesh
from jax.sharding import PartitionSpec as P

CHIPS = ("y", "z")
RANK = 32
HIGHEST = lax.Precision.HIGHEST
F32 = jnp.float32
BF16 = jnp.bfloat16
VMEM = pl.BlockSpec(memory_space=pltpu.VMEM)
NT = (((1,), (1,)), ((), ()))
TN = (((0,), (0,)), ((), ()))


def kernel_call(body, outs, flops, moved, *args):
    return pl.pallas_call(
        body,
        out_shape=outs,
        in_specs=[VMEM] * len(args),
        out_specs=jax.tree.map(lambda _: VMEM, outs),
        compiler_params=pltpu.CompilerParams(vmem_limit_bytes=24 << 20),
        cost_estimate=pl.CostEstimate(flops=flops, bytes_accessed=moved, transcendentals=0),
    )(*args)


def lanes_of(shape):
    return lax.broadcasted_iota(jnp.int32, shape, len(shape) - 1)


def pack_square(square):
    lane = lanes_of((8, 128))
    out = jnp.where(lane < 32, square[0:8], 0.0)
    for q in range(1, 4):
        block = pltpu.roll(square[8 * q : 8 * q + 8], 32 * q, axis=1)
        out = jnp.where((lane >= 32 * q) & (lane < 32 * q + 32), block, out)
    return out


def unpack_square(tile):
    return jnp.concatenate([tile] + [pltpu.roll(tile, 128 - 32 * q, axis=1) for q in range(1, 4)])


def pack_lower(square):
    lane = lanes_of((8, 128))
    out = jnp.where(lane < 32, square[24:32], 0.0)
    for at, width, first in ((32, 24, 16), (56, 16, 8), (72, 8, 0)):
        block = pltpu.roll(square[first : first + 8], at, axis=1)
        out = jnp.where((lane >= at) & (lane < at + width), block, out)
    return out


def unpack_lower(tile):
    lower = jnp.concatenate([pltpu.roll(tile, 128 - at, axis=1) for at in (72, 56, 32)] + [tile])
    lane = lanes_of((RANK, 128))
    row = lax.broadcasted_iota(jnp.int32, (RANK, 128), 0)
    lower = jnp.where(lane <= row, lower, 0.0)
    turned = jnp.concatenate([lower, jnp.zeros((128 - RANK, 128), F32)]).T[:RANK]
    return jnp.where(lane <= row, lower, turned)


def inverse_factor(gram):
    lane = lanes_of((RANK, 128))
    row = lax.broadcasted_iota(jnp.int32, (RANK, 128), 0)
    work = jnp.where(lane < RANK, gram, jnp.where(lane == row + RANK, 1.0, 0.0))
    pivots = jnp.ones((RANK, 128), F32)
    width = 8
    for start in range(0, RANK, width):
        columns = [
            jnp.broadcast_to(work[:, start + i : start + i + 1], (RANK, 128)) for i in range(width)
        ]
        for i in range(width):
            k = start + i
            pivot = jnp.broadcast_to(columns[i][k : k + 1], (RANK, 128))
            pivots = jnp.where(row == k, pivot, pivots)
            factor = jnp.where(row > k, columns[i] / pivot, 0.0)
            for later in range(i + 1, width):
                columns[later] = columns[later] - factor * columns[later][k : k + 1]
            work = work - factor * work[k : k + 1]
    return (work / jnp.sqrt(pivots))[:, RANK : 2 * RANK]


def fan_out(panel_ref, out_ref):
    panel = jnp.concatenate([panel_ref[...].astype(F32), jnp.zeros((RANK, 128 - RANK), F32)], axis=1)
    tile = pack_square(panel).astype(BF16)
    for copy in range(out_ref.shape[0]):
        out_ref[copy] = tile


def first_sketch(tiles_ref, transport_ref, out_ref):
    cores, chips = tiles_ref.shape[:2]
    cols = transport_ref.shape[1]
    lane = lanes_of((8, 128))
    masks = [(lane >= 32 * q) & (lane < 32 * q + 32) for q in range(4)]
    total = jnp.zeros((transport_ref.shape[0], 128), F32)
    group = 8
    for start in range(0, chips, group):
        rows = []
        for chip in range(start, start + group):
            for core in range(cores):
                tile = tiles_ref[core, chip].astype(F32)
                rows += [jnp.where(mask, tile, 0.0) for mask in masks]
        at = start * (cols // chips)
        total += jnp.dot(
            transport_ref[:, at : at + group * (cols // chips)],
            jnp.concatenate(rows).astype(BF16),
            preferred_element_type=F32,
        )
    turned = total.T
    sketch = (turned[0:32] + turned[32:64]) + (turned[64:96] + turned[96:128])
    for copy in range(out_ref.shape[0]):
        out_ref[copy] = sketch


def next_sketch(panel_ref, transport_ref, out_ref):
    groups, _, width = panel_ref.shape
    sketch = jnp.zeros((RANK, transport_ref.shape[0]), F32)
    for g in range(groups):
        sketch += lax.dot_general(
            panel_ref[g],
            transport_ref[:, g * width : (g + 1) * width],
            NT,
            preferred_element_type=F32,
        )
    for copy in range(out_ref.shape[0]):
        out_ref[copy] = sketch


def product(parts_ref, transport_ref):
    sketch = (parts_ref[0] + parts_ref[1]) + (parts_ref[2] + parts_ref[3])
    gram = lax.dot_general(sketch, sketch, NT, precision=HIGHEST, preferred_element_type=F32)
    gram = jnp.concatenate([gram, jnp.zeros((RANK, 128 - RANK), F32)], axis=1)
    high = sketch.astype(BF16)
    low = (sketch - high.astype(F32)).astype(BF16)
    both = jnp.concatenate([high, low])

    def columns(at, width):
        out = jnp.dot(both, transport_ref[:, at : at + width], preferred_element_type=F32)
        return out[:RANK] + out[RANK:]

    return sketch, pack_lower(gram), columns


def middle_product(parts_ref, transport_ref, out_ref):
    cores, groups, height, _ = out_ref.shape
    tiles = height // 8 - 1
    width = tiles // 4 * 128
    _, gram, columns = product(parts_ref, transport_ref)
    for core in range(cores):
        for g in range(groups):
            block = columns((core * groups + g) * width, width)
            for t in range(tiles):
                a, c = t % 4, t // 4
                out_ref[core, g, 8 * t : 8 * t + 8] = block[8 * a : 8 * a + 8, 128 * c : 128 * c + 128]
            out_ref[core, g, 8 * tiles : height] = gram


def last_product(parts_ref, transport_ref, out_ref, sketch_ref):
    cores, chips, _, _ = out_ref.shape
    sketch, gram, columns = product(parts_ref, transport_ref)
    sketch_ref[...] = sketch
    lane = lanes_of((8, 128))
    low_half, even = lane < 64, lane % 64 < 32
    for wide in range(chips // 8):
        block = columns(512 * wide, 512)
        for c in range(4):
            t = [block[8 * a : 8 * a + 8, 128 * c : 128 * c + 128] for a in range(4)]
            u = [None] * 4
            for a in (0, 1):
                u[a] = jnp.where(low_half, t[a], pltpu.roll(t[a + 2], 64, axis=1))
                u[a + 2] = jnp.where(low_half, pltpu.roll(t[a], 64, axis=1), t[a + 2])
            for a in (0, 2):
                v0 = jnp.where(even, u[a], pltpu.roll(u[a + 1], 32, axis=1))
                v1 = jnp.where(even, pltpu.roll(u[a], 96, axis=1), u[a + 1])
                for b, v in ((a, v0), (a + 1, v1)):
                    device = 16 * wide + 4 * c + b
                    out_ref[device % 2, device // 2, 0:8] = v
    for core in range(cores):
        for chip in range(chips):
            out_ref[core, chip, 8:16] = gram


def encode(total):
    lane = lanes_of((8, 128))
    gram = total[-8:]
    terms = []
    for _ in range(3):
        terms.append(gram.astype(BF16).astype(F32))
        gram = gram - terms[-1]
    middle = pltpu.roll(terms[1], 80, axis=1)
    first = jnp.where(lane < 80, terms[0], middle)
    second = jnp.where(lane < 32, middle, pltpu.roll(terms[2], 32, axis=1))
    return jnp.concatenate([total[:-8], first, second]).astype(BF16)


def decoded_sum(messages_ref):
    total = messages_ref[0].astype(F32)
    for p in range(1, messages_ref.shape[0]):
        total = total + messages_ref[p].astype(F32)
    lane = lanes_of((8, 128))
    first, second = total[-16:-8], total[-8:]
    middle = pltpu.roll(jnp.where(lane < 32, second, first), 48, axis=1)
    gram = (pltpu.roll(second, 96, axis=1) + middle) + first
    return jnp.concatenate([total[:-16], jnp.where(lane < 80, gram, 0.0)])


def add_cores(sums_ref, out_ref):
    for peer in range(out_ref.shape[0]):
        out_ref[peer] = encode(sums_ref[0, peer] + sums_ref[1, peer])


def add_peers(messages_ref, out_ref):
    message = encode(decoded_sum(messages_ref))
    for copy in range(out_ref.shape[0]):
        out_ref[copy] = message


def normalise(total_rows, messages_ref, out_ref):
    total = decoded_sum(messages_ref)
    tiles = total.shape[0] // 8 - 1
    inverse = inverse_factor(unpack_lower(total[8 * tiles :]) / total_rows)
    for c in range(tiles // 4):
        block = total[32 * c : 32 * c + 32]
        panel = jnp.dot(inverse, block, precision=HIGHEST, preferred_element_type=F32).astype(BF16)
        for copy in range(out_ref.shape[0]):
            out_ref[copy, :, 128 * c : 128 * c + 128] = panel


def finish(total_rows, messages_ref, sketch_ref, basis_ref, coimage_ref):
    total = decoded_sum(messages_ref)
    inverse = inverse_factor(unpack_lower(total[8:]) / total_rows)
    basis_ref[...] = jnp.dot(
        inverse, sketch_ref[...], precision=HIGHEST, preferred_element_type=F32
    )
    block = unpack_square(total[0:8])[:, :RANK]
    coimage_ref[...] = lax.dot_general(
        block, inverse, (((0,), (1,)), ((), ())), precision=HIGHEST, preferred_element_type=F32
    )


def on_device(transport, test_panel):
    rows, cols = transport.shape
    total_rows = rows * lax.axis_size(("y", "z", "core"))
    ny, nz, nx = (lax.axis_size(name) for name in ("y", "z", "x"))
    chips = ny * nz
    flops = 2 * rows * cols * 128
    shape = jax.ShapeDtypeStruct

    copies = kernel_call(fan_out, shape((chips, 8, 128), BF16), 1 << 32, 8 << 20, test_panel)
    tiles = lax.all_to_all(copies, CHIPS, 0, 0)
    tiles = lax.all_to_all(jnp.broadcast_to(tiles, (2, chips, 8, 128)), "core", 0, 0)
    partial = kernel_call(
        first_sketch, shape((nx, RANK, rows), F32), flops, 5 << 20, tiles, transport
    )
    parts = lax.all_to_all(partial, "x", 0, 0)

    width = cols // (2 * ny)
    height = RANK * width // 128 + 8
    sums = kernel_call(
        middle_product, shape((2, ny, height, 128), F32), flops, 5 << 20, parts, transport
    )
    sums = lax.all_to_all(sums, "core", 0, 0)
    sums = kernel_call(add_cores, shape((ny, height + 8, 128), BF16), 0, 1 << 20, sums)
    sums = lax.all_to_all(sums, "y", 0, 0)
    sums = kernel_call(add_peers, shape((nz, height + 8, 128), BF16), 0, 1 << 20, sums)
    sums = lax.all_to_all(sums, "z", 0, 0)
    panel = kernel_call(
        functools.partial(normalise, total_rows),
        shape((2 * ny, RANK, width), BF16),
        1 << 32,
        8 << 20,
        sums,
    )
    panel = lax.all_to_all(panel, ("core", "y"), 0, 0)
    partial = kernel_call(
        next_sketch,
        shape((nx, RANK, rows), F32),
        flops,
        5 << 20,
        panel,
        transport,
    )
    parts = lax.all_to_all(partial, "x", 0, 0)

    sums, sketch = kernel_call(
        last_product,
        (shape((2, chips, 16, 128), F32), shape((RANK, rows), F32)),
        flops,
        6 << 20,
        parts,
        transport,
    )
    sums = lax.all_to_all(sums, "core", 0, 0)
    sums = kernel_call(add_cores, shape((chips, 24, 128), BF16), 0, 1 << 20, sums)
    sums = lax.all_to_all(sums, CHIPS, 0, 0)
    basis, coimage = kernel_call(
        functools.partial(finish, total_rows),
        (shape((RANK, rows), F32), shape((RANK, RANK), F32)),
        1 << 20,
        1 << 20,
        sums,
        sketch,
    )
    return (basis.T, coimage)


def solution(mesh):
    sizes = {"cam": (("y", 8), ("z", 8), ("core", 2)), "proj": (("x", 4),)}
    names = [name for axis in mesh.axis_names for name, _ in sizes[axis]]
    shape = [size for axis in mesh.axis_names for _, size in sizes[axis]]
    fine = Mesh(np.asarray(mesh.devices).reshape(shape), names)
    rows = ("y", "z", "core")
    return jax.shard_map(
        on_device,
        mesh=fine,
        in_specs=(P(rows, "x"), P(("x",) + rows, None)),
        out_specs=(P(rows, None), P(("x",) + rows, None)),
        check_vma=False,
    )
```

```python
import functools

import jax
import jax.numpy as jnp
import numpy as np
from jax import lax
from jax.experimental import pallas as pl
from jax.experimental.pallas import tpu as pltpu
from jax.sharding import Mesh
from jax.sharding import PartitionSpec as P

CHIPS = ("y", "z")
RANK = 32
HIGHEST = lax.Precision.HIGHEST
F32 = jnp.float32
BF16 = jnp.bfloat16
VMEM = pl.BlockSpec(memory_space=pltpu.VMEM)
NT = (((1,), (1,)), ((), ()))
TN = (((0,), (0,)), ((), ()))


def kernel_call(body, outs, flops, moved, *args):
    return pl.pallas_call(
        body,
        out_shape=outs,
        in_specs=[VMEM] * len(args),
        out_specs=jax.tree.map(lambda _: VMEM, outs),
        compiler_params=pltpu.CompilerParams(vmem_limit_bytes=24 << 20),
        cost_estimate=pl.CostEstimate(flops=flops, bytes_accessed=moved, transcendentals=0),
    )(*args)


def lanes_of(shape):
    return lax.broadcasted_iota(jnp.int32, shape, len(shape) - 1)


def pack_square(square):
    lane = lanes_of((8, 128))
    out = jnp.where(lane < 32, square[0:8], 0.0)
    for q in range(1, 4):
        block = pltpu.roll(square[8 * q : 8 * q + 8], 32 * q, axis=1)
        out = jnp.where((lane >= 32 * q) & (lane < 32 * q + 32), block, out)
    return out


def unpack_square(tile):
    return jnp.concatenate([tile] + [pltpu.roll(tile, 128 - 32 * q, axis=1) for q in range(1, 4)])


def pack_lower(square):
    lane = lanes_of((8, 128))
    out = jnp.where(lane < 32, square[24:32], 0.0)
    for at, width, first in ((32, 24, 16), (56, 16, 8), (72, 8, 0)):
        block = pltpu.roll(square[first : first + 8], at, axis=1)
        out = jnp.where((lane >= at) & (lane < at + width), block, out)
    return out


def unpack_lower(tile):
    lower = jnp.concatenate([pltpu.roll(tile, 128 - at, axis=1) for at in (72, 56, 32)] + [tile])
    lane = lanes_of((RANK, 128))
    row = lax.broadcasted_iota(jnp.int32, (RANK, 128), 0)
    lower = jnp.where(lane <= row, lower, 0.0)
    turned = jnp.concatenate([lower, jnp.zeros((128 - RANK, 128), F32)]).T[:RANK]
    return jnp.where(lane <= row, lower, turned)


def inverse_factor(gram):
    lane = lanes_of((RANK, 128))
    row = lax.broadcasted_iota(jnp.int32, (RANK, 128), 0)
    work = jnp.where(lane < RANK, gram, jnp.where(lane == row + RANK, 1.0, 0.0))
    pivots = jnp.ones((RANK, 128), F32)
    width = 16
    for start in range(0, RANK, width):
        columns = [
            jnp.broadcast_to(work[:, start + i : start + i + 1], (RANK, 128)) for i in range(width)
        ]
        for i in range(width):
            k = start + i
            pivot = jnp.broadcast_to(columns[i][k : k + 1], (RANK, 128))
            pivots = jnp.where(row == k, pivot, pivots)
            factor = jnp.where(row > k, columns[i] / pivot, 0.0)
            for later in range(i + 1, width):
                columns[later] = columns[later] - factor * columns[later][k : k + 1]
            work = work - factor * work[k : k + 1]
    return (work / jnp.sqrt(pivots))[:, RANK : 2 * RANK]


def fan_out(panel_ref, out_ref):
    panel = jnp.concatenate([panel_ref[...].astype(F32), jnp.zeros((RANK, 128 - RANK), F32)], axis=1)
    tile = pack_square(panel).astype(BF16)
    for copy in range(out_ref.shape[0]):
        out_ref[copy] = tile


def first_sketch(tiles_ref, transport_ref, out_ref):
    cores, chips = tiles_ref.shape[:2]
    cols = transport_ref.shape[1]
    lane = lanes_of((8, 128))
    masks = [(lane >= 32 * q) & (lane < 32 * q + 32) for q in range(4)]
    total = jnp.zeros((transport_ref.shape[0], 128), F32)
    group = 8
    for start in range(0, chips, group):
        rows = []
        for chip in range(start, start + group):
            for core in range(cores):
                tile = tiles_ref[core, chip].astype(F32)
                rows += [jnp.where(mask, tile, 0.0) for mask in masks]
        at = start * (cols // chips)
        total += jnp.dot(
            transport_ref[:, at : at + group * (cols // chips)],
            jnp.concatenate(rows).astype(BF16),
            preferred_element_type=F32,
        )
    turned = total.T
    sketch = (turned[0:32] + turned[32:64]) + (turned[64:96] + turned[96:128])
    for copy in range(out_ref.shape[0]):
        out_ref[copy] = sketch


def next_sketch(panel_ref, transport_ref, out_ref):
    groups, _, width = panel_ref.shape
    sketch = jnp.zeros((RANK, transport_ref.shape[0]), F32)
    for g in range(groups):
        sketch += lax.dot_general(
            panel_ref[g],
            transport_ref[:, g * width : (g + 1) * width],
            NT,
            preferred_element_type=F32,
        )
    for copy in range(out_ref.shape[0]):
        out_ref[copy] = sketch


def product(parts_ref, transport_ref):
    sketch = (parts_ref[0] + parts_ref[1]) + (parts_ref[2] + parts_ref[3])
    gram = lax.dot_general(sketch, sketch, NT, precision=HIGHEST, preferred_element_type=F32)
    gram = jnp.concatenate([gram, jnp.zeros((RANK, 128 - RANK), F32)], axis=1)
    high = sketch.astype(BF16)
    low = (sketch - high.astype(F32)).astype(BF16)
    both = jnp.concatenate([high, low])

    def columns(at, width):
        out = jnp.dot(both, transport_ref[:, at : at + width], preferred_element_type=F32)
        return out[:RANK] + out[RANK:]

    return sketch, pack_lower(gram), columns


def middle_product(groups, parts_ref, transport_ref, out_ref):
    cores, height, _ = out_ref.shape
    cols = transport_ref.shape[1]
    width = cols // (cores * groups)
    _, gram, columns = product(parts_ref, transport_ref)
    for group in range(groups):
        for core in range(cores):
            block = columns((group * cores + core) * width, width)
            for t in range(width // 32):
                a, c = t % 4, t // 4
                at = group * width // 4 + 8 * t
                out_ref[core, at : at + 8] = block[8 * a : 8 * a + 8, 128 * c : 128 * c + 128]
    for core in range(cores):
        out_ref[core, height - 8 : height] = gram


def last_product(parts_ref, transport_ref, out_ref, sketch_ref):
    cores, height, _ = out_ref.shape
    chips = height // 8 - 1
    sketch, gram, columns = product(parts_ref, transport_ref)
    sketch_ref[...] = sketch
    lane = lanes_of((8, 128))
    low_half, even = lane < 64, lane % 64 < 32
    for wide in range(chips // 8):
        block = columns(512 * wide, 512)
        for c in range(4):
            t = [block[8 * a : 8 * a + 8, 128 * c : 128 * c + 128] for a in range(4)]
            u = [None] * 4
            for a in (0, 1):
                u[a] = jnp.where(low_half, t[a], pltpu.roll(t[a + 2], 64, axis=1))
                u[a + 2] = jnp.where(low_half, pltpu.roll(t[a], 64, axis=1), t[a + 2])
            for a in (0, 2):
                v0 = jnp.where(even, u[a], pltpu.roll(u[a + 1], 32, axis=1))
                v1 = jnp.where(even, pltpu.roll(u[a], 96, axis=1), u[a + 1])
                for b, v in ((a, v0), (a + 1, v1)):
                    device = 16 * wide + 4 * c + b
                    y, z = divmod(device // 2, 8)
                    at = 8 * (z * (chips // 8) + y)
                    out_ref[device % 2, at : at + 8] = v
    for core in range(cores):
        out_ref[core, height - 8 : height] = gram


def three_terms(gram):
    lane = lanes_of((8, 128))
    terms = []
    for _ in range(3):
        terms.append(gram.astype(BF16).astype(F32))
        gram = gram - terms[-1]
    middle = pltpu.roll(terms[1], 80, axis=1)
    first = jnp.where(lane < 80, terms[0], middle)
    second = jnp.where(lane < 32, middle, pltpu.roll(terms[2], 32, axis=1))
    return jnp.concatenate([first, second])


def decoded_sum(messages_ref):
    total = messages_ref[0].astype(F32)
    for p in range(1, messages_ref.shape[0]):
        total = total + messages_ref[p].astype(F32)
    lane = lanes_of((8, 128))
    first, second = total[-16:-8], total[-8:]
    middle = pltpu.roll(jnp.where(lane < 32, second, first), 48, axis=1)
    gram = (pltpu.roll(second, 96, axis=1) + middle) + first
    return jnp.concatenate([total[:-16], jnp.where(lane < 80, gram, 0.0)])


def add_cores(sums_ref, out_ref):
    peers, height, _ = out_ref.shape
    rows = height - 16
    gram = three_terms(sums_ref[0, peers * rows :] + sums_ref[1, peers * rows :])
    for peer in range(peers):
        at = slice(peer * rows, (peer + 1) * rows)
        block = sums_ref[0, at] + sums_ref[1, at]
        out_ref[peer] = jnp.concatenate([block, gram]).astype(BF16)


def add_peers(messages_ref, out_ref):
    total = decoded_sum(messages_ref)
    message = jnp.concatenate([total[:-8], three_terms(total[-8:])]).astype(BF16)
    for copy in range(out_ref.shape[0]):
        out_ref[copy] = message


def normalise(total_rows, messages_ref, out_ref):
    total = decoded_sum(messages_ref)
    tiles = total.shape[0] // 8 - 1
    inverse = inverse_factor(unpack_lower(total[8 * tiles :]) / total_rows)
    for c in range(tiles // 4):
        block = total[32 * c : 32 * c + 32]
        panel = jnp.dot(inverse, block, precision=HIGHEST, preferred_element_type=F32).astype(BF16)
        for copy in range(out_ref.shape[0]):
            out_ref[copy, :, 128 * c : 128 * c + 128] = panel


def finish(total_rows, messages_ref, sketch_ref, basis_ref, coimage_ref):
    total = decoded_sum(messages_ref)
    inverse = inverse_factor(unpack_lower(total[8:]) / total_rows)
    basis_ref[...] = jnp.dot(
        inverse, sketch_ref[...], precision=HIGHEST, preferred_element_type=F32
    )
    block = unpack_square(total[0:8])[:, :RANK]
    coimage_ref[...] = lax.dot_general(
        block, inverse, (((0,), (1,)), ((), ())), precision=HIGHEST, preferred_element_type=F32
    )


def on_device(transport, test_panel):
    rows, cols = transport.shape
    total_rows = rows * lax.axis_size(("y", "z", "core"))
    ny, nz, nx = (lax.axis_size(name) for name in ("y", "z", "x"))
    chips = ny * nz
    flops = 2 * rows * cols * 128
    shape = jax.ShapeDtypeStruct

    copies = kernel_call(fan_out, shape((chips, 8, 128), BF16), 1 << 32, 8 << 20, test_panel)
    tiles = lax.all_to_all(copies, CHIPS, 0, 0)
    tiles = lax.all_to_all(jnp.broadcast_to(tiles, (2, chips, 8, 128)), "core", 0, 0)
    partial = kernel_call(
        first_sketch, shape((nx, RANK, rows), F32), flops, 5 << 20, tiles, transport
    )
    parts = lax.all_to_all(partial, "x", 0, 0)

    width = cols // (2 * ny)
    height = RANK * width // 128
    sums = kernel_call(
        functools.partial(middle_product, ny), shape((2, ny * height + 8, 128), F32), flops, 5 << 20, parts, transport
    )
    sums = lax.all_to_all(sums, "core", 0, 0)
    sums = kernel_call(add_cores, shape((ny, height + 16, 128), BF16), 0, 1 << 20, sums)
    sums = lax.all_to_all(sums, "y", 0, 0)
    sums = kernel_call(add_peers, shape((nz, height + 16, 128), BF16), 0, 1 << 20, sums)
    sums = lax.all_to_all(sums, "z", 0, 0)
    panel = kernel_call(
        functools.partial(normalise, total_rows),
        shape((2 * ny, RANK, width), BF16),
        1 << 32,
        8 << 20,
        sums,
    )
    panel = lax.all_to_all(panel, ("y", "core"), 0, 0)
    partial = kernel_call(
        next_sketch,
        shape((nx, RANK, rows), F32),
        flops,
        5 << 20,
        panel,
        transport,
    )
    parts = lax.all_to_all(partial, "x", 0, 0)

    sums, sketch = kernel_call(
        last_product,
        (shape((2, 8 * chips + 8, 128), F32), shape((RANK, rows), F32)),
        flops,
        6 << 20,
        parts,
        transport,
    )
    sums = lax.all_to_all(sums, "core", 0, 0)
    sums = kernel_call(add_cores, shape((chips, 24, 128), BF16), 0, 1 << 20, sums)
    sums = lax.all_to_all(sums, ("z", "y"), 0, 0)
    basis, coimage = kernel_call(
        functools.partial(finish, total_rows),
        (shape((RANK, rows), F32), shape((RANK, RANK), F32)),
        1 << 20,
        1 << 20,
        sums,
        sketch,
    )
    return (basis.T, coimage)


def solution(mesh):
    sizes = {"cam": (("y", 8), ("z", 8), ("core", 2)), "proj": (("x", 4),)}
    names = [name for axis in mesh.axis_names for name, _ in sizes[axis]]
    shape = [size for axis in mesh.axis_names for _, size in sizes[axis]]
    fine = Mesh(np.asarray(mesh.devices).reshape(shape), names)
    rows = ("y", "z", "core")
    return jax.shard_map(
        on_device,
        mesh=fine,
        in_specs=(P(rows, "x"), P(("x",) + rows, None)),
        out_specs=(P(rows, None), P(("x",) + rows, None)),
        check_vma=False,
    )
```

```python
import functools

import jax
import jax.numpy as jnp
import numpy as np
from jax import lax
from jax.experimental import pallas as pl
from jax.experimental.pallas import tpu as pltpu
from jax.sharding import Mesh
from jax.sharding import PartitionSpec as P

RANK = 32
HIGHEST = lax.Precision.HIGHEST
F32 = jnp.float32
BF16 = jnp.bfloat16
VMEM = pl.BlockSpec(memory_space=pltpu.VMEM)
NT = (((1,), (1,)), ((), ()))
TN = (((0,), (0,)), ((), ()))


def kernel_call(body, outs, flops, moved, *args):
    return pl.pallas_call(
        body,
        out_shape=outs,
        in_specs=[VMEM] * len(args),
        out_specs=jax.tree.map(lambda _: VMEM, outs),
        compiler_params=pltpu.CompilerParams(vmem_limit_bytes=24 << 20),
        cost_estimate=pl.CostEstimate(flops=flops, bytes_accessed=moved, transcendentals=0),
    )(*args)


def lanes_of(shape):
    return lax.broadcasted_iota(jnp.int32, shape, len(shape) - 1)


def pack_square(square):
    lane = lanes_of((8, 128))
    out = jnp.where(lane < 32, square[0:8], 0.0)
    for q in range(1, 4):
        block = pltpu.roll(square[8 * q : 8 * q + 8], 32 * q, axis=1)
        out = jnp.where((lane >= 32 * q) & (lane < 32 * q + 32), block, out)
    return out


def unpack_square(tile):
    return jnp.concatenate([tile] + [pltpu.roll(tile, 128 - 32 * q, axis=1) for q in range(1, 4)])


def pack_lower(square):
    lane = lanes_of((8, 128))
    out = jnp.where(lane < 32, square[24:32], 0.0)
    for at, width, first in ((32, 24, 16), (56, 16, 8), (72, 8, 0)):
        block = pltpu.roll(square[first : first + 8], at, axis=1)
        out = jnp.where((lane >= at) & (lane < at + width), block, out)
    return out


def unpack_lower(tile):
    lower = jnp.concatenate([pltpu.roll(tile, 128 - at, axis=1) for at in (72, 56, 32)] + [tile])
    lane = lanes_of((RANK, 128))
    row = lax.broadcasted_iota(jnp.int32, (RANK, 128), 0)
    lower = jnp.where(lane <= row, lower, 0.0)
    turned = jnp.concatenate([lower, jnp.zeros((128 - RANK, 128), F32)]).T[:RANK]
    return jnp.where(lane <= row, lower, turned)


def inverse_factor(gram):
    lane = lanes_of((RANK, 128))
    row = lax.broadcasted_iota(jnp.int32, (RANK, 128), 0)
    work = jnp.where(lane < RANK, gram, jnp.where(lane == row + RANK, 1.0, 0.0))
    pivots = jnp.ones((RANK, 128), F32)
    width = 16
    for start in range(0, RANK, width):
        columns = [
            jnp.broadcast_to(work[:, start + i : start + i + 1], (RANK, 128)) for i in range(width)
        ]
        for i in range(width):
            k = start + i
            pivot = jnp.broadcast_to(columns[i][k : k + 1], (RANK, 128))
            pivots = jnp.where(row == k, pivot, pivots)
            factor = jnp.where(row > k, columns[i] / pivot, 0.0)
            for later in range(i + 1, width):
                columns[later] = columns[later] - factor * columns[later][k : k + 1]
            work = work - factor * work[k : k + 1]
    return (work / jnp.sqrt(pivots))[:, RANK : 2 * RANK]


def fan_out(panel_ref, out_ref):
    panel = jnp.concatenate([panel_ref[...].astype(F32), jnp.zeros((RANK, 128 - RANK), F32)], axis=1)
    tile = pack_square(panel).astype(BF16)
    for copy in range(out_ref.shape[0]):
        out_ref[copy] = tile


def first_sketch(tiles_ref, transport_ref, out_ref):
    cores, chips = 2, tiles_ref.shape[0] // 2
    cols = transport_ref.shape[1]
    lane = lanes_of((8, 128))
    masks = [(lane >= 32 * q) & (lane < 32 * q + 32) for q in range(4)]
    total = jnp.zeros((transport_ref.shape[0], 128), F32)
    group = 8
    for start in range(0, chips, group):
        rows = []
        for chip in range(start, start + group):
            for core in range(cores):
                y, z = divmod(chip, 8)
                tile = tiles_ref[core * chips + z * (chips // 8) + y].astype(F32)
                rows += [jnp.where(mask, tile, 0.0) for mask in masks]
        at = start * (cols // chips)
        total += jnp.dot(
            transport_ref[:, at : at + group * (cols // chips)],
            jnp.concatenate(rows).astype(BF16),
            preferred_element_type=F32,
        )
    turned = total.T
    sketch = (turned[0:32] + turned[32:64]) + (turned[64:96] + turned[96:128])
    for copy in range(out_ref.shape[0]):
        out_ref[copy] = sketch


def next_sketch(panel_ref, transport_ref, out_ref):
    groups, _, width = panel_ref.shape
    sketch = jnp.zeros((RANK, transport_ref.shape[0]), F32)
    for g in range(groups):
        sketch += lax.dot_general(
            panel_ref[g],
            transport_ref[:, g * width : (g + 1) * width],
            NT,
            preferred_element_type=F32,
        )
    for copy in range(out_ref.shape[0]):
        out_ref[copy] = sketch


def product(parts_ref, transport_ref):
    sketch = (parts_ref[0] + parts_ref[1]) + (parts_ref[2] + parts_ref[3])
    gram = lax.dot_general(sketch, sketch, NT, precision=HIGHEST, preferred_element_type=F32)
    gram = jnp.concatenate([gram, jnp.zeros((RANK, 128 - RANK), F32)], axis=1)
    high = sketch.astype(BF16)
    low = (sketch - high.astype(F32)).astype(BF16)
    both = jnp.concatenate([high, low])

    def columns(at, width):
        out = jnp.dot(both, transport_ref[:, at : at + width], preferred_element_type=F32)
        return out[:RANK] + out[RANK:]

    return sketch, pack_lower(gram), columns


def middle_product(groups, parts_ref, transport_ref, out_ref):
    cores, height, _ = out_ref.shape
    cols = transport_ref.shape[1]
    width = cols // (cores * groups)
    _, gram, columns = product(parts_ref, transport_ref)
    for group in range(groups):
        for core in range(cores):
            block = columns((core * groups + group) * width, width)
            for t in range(width // 32):
                a, c = t % 4, t // 4
                at = group * width // 4 + 8 * t
                out_ref[core, at : at + 8] = block[8 * a : 8 * a + 8, 128 * c : 128 * c + 128]
    for core in range(cores):
        out_ref[core, height - 8 : height] = gram


def last_product(parts_ref, transport_ref, out_ref, sketch_ref):
    cores, height, _ = out_ref.shape
    chips = height // 8 - 1
    sketch, gram, columns = product(parts_ref, transport_ref)
    sketch_ref[...] = sketch
    lane = lanes_of((8, 128))
    low_half, even = lane < 64, lane % 64 < 32
    for wide in range(chips // 8):
        block = columns(512 * wide, 512)
        for c in range(4):
            t = [block[8 * a : 8 * a + 8, 128 * c : 128 * c + 128] for a in range(4)]
            u = [None] * 4
            for a in (0, 1):
                u[a] = jnp.where(low_half, t[a], pltpu.roll(t[a + 2], 64, axis=1))
                u[a + 2] = jnp.where(low_half, pltpu.roll(t[a], 64, axis=1), t[a + 2])
            for a in (0, 2):
                v0 = jnp.where(even, u[a], pltpu.roll(u[a + 1], 32, axis=1))
                v1 = jnp.where(even, pltpu.roll(u[a], 96, axis=1), u[a + 1])
                for b, v in ((a, v0), (a + 1, v1)):
                    device = 16 * wide + 4 * c + b
                    y, z = divmod(device // 2, 8)
                    at = 8 * (z * (chips // 8) + y)
                    out_ref[device % 2, at : at + 8] = v
    for core in range(cores):
        out_ref[core, height - 8 : height] = gram


def three_terms(gram):
    lane = lanes_of((8, 128))
    terms = []
    for _ in range(3):
        terms.append(gram.astype(BF16).astype(F32))
        gram = gram - terms[-1]
    middle = pltpu.roll(terms[1], 80, axis=1)
    first = jnp.where(lane < 80, terms[0], middle)
    second = jnp.where(lane < 32, middle, pltpu.roll(terms[2], 32, axis=1))
    return jnp.concatenate([first, second])


def decoded_sum(messages_ref):
    total = messages_ref[0].astype(F32)
    for p in range(1, messages_ref.shape[0]):
        total = total + messages_ref[p].astype(F32)
    lane = lanes_of((8, 128))
    first, second = total[-16:-8], total[-8:]
    middle = pltpu.roll(jnp.where(lane < 32, second, first), 48, axis=1)
    gram = (pltpu.roll(second, 96, axis=1) + middle) + first
    return jnp.concatenate([total[:-16], jnp.where(lane < 80, gram, 0.0)])


def add_cores(sums_ref, out_ref):
    peers, height, _ = out_ref.shape
    rows = height - 16
    gram = three_terms(sums_ref[0, peers * rows :] + sums_ref[1, peers * rows :])
    for peer in range(peers):
        at = slice(peer * rows, (peer + 1) * rows)
        block = sums_ref[0, at] + sums_ref[1, at]
        out_ref[peer] = jnp.concatenate([block, gram]).astype(BF16)


def add_peers(messages_ref, out_ref):
    total = decoded_sum(messages_ref)
    message = jnp.concatenate([total[:-8], three_terms(total[-8:])]).astype(BF16)
    for copy in range(out_ref.shape[0]):
        out_ref[copy] = message


def normalise(total_rows, messages_ref, out_ref):
    total = decoded_sum(messages_ref)
    tiles = total.shape[0] // 8 - 1
    inverse = inverse_factor(unpack_lower(total[8 * tiles :]) / total_rows)
    for c in range(tiles // 4):
        block = total[32 * c : 32 * c + 32]
        panel = jnp.dot(inverse, block, precision=HIGHEST, preferred_element_type=F32).astype(BF16)
        for copy in range(out_ref.shape[0]):
            out_ref[copy, :, 128 * c : 128 * c + 128] = panel


def finish(total_rows, messages_ref, sketch_ref, basis_ref, coimage_ref):
    total = decoded_sum(messages_ref)
    inverse = inverse_factor(unpack_lower(total[8:]) / total_rows)
    basis_ref[...] = jnp.dot(
        inverse, sketch_ref[...], precision=HIGHEST, preferred_element_type=F32
    )
    block = unpack_square(total[0:8])[:, :RANK]
    coimage_ref[...] = lax.dot_general(
        block, inverse, (((0,), (1,)), ((), ())), precision=HIGHEST, preferred_element_type=F32
    )


def on_device(transport, test_panel):
    rows, cols = transport.shape
    total_rows = rows * lax.axis_size(("y", "z", "core"))
    ny, nz, nx = (lax.axis_size(name) for name in ("y", "z", "x"))
    chips = ny * nz
    flops = 2 * rows * cols * 128
    shape = jax.ShapeDtypeStruct

    copies = kernel_call(fan_out, shape((2 * chips, 8, 128), BF16), 1 << 32, 8 << 20, test_panel)
    tiles = lax.all_to_all(copies, ("core", "z", "y"), 0, 0)
    partial = kernel_call(
        first_sketch, shape((nx, RANK, rows), F32), flops, 5 << 20, tiles, transport
    )
    parts = lax.all_to_all(partial, "x", 0, 0)

    width = cols // (2 * ny)
    height = RANK * width // 128
    sums = kernel_call(
        functools.partial(middle_product, ny), shape((2, ny * height + 8, 128), F32), flops, 5 << 20, parts, transport
    )
    sums = lax.all_to_all(sums, "core", 0, 0)
    sums = kernel_call(add_cores, shape((ny, height + 16, 128), BF16), 0, 1 << 20, sums)
    sums = lax.all_to_all(sums, "y", 0, 0)
    sums = kernel_call(add_peers, shape((nz, height + 16, 128), BF16), 0, 1 << 20, sums)
    sums = lax.all_to_all(sums, "z", 0, 0)
    panel = kernel_call(
        functools.partial(normalise, total_rows),
        shape((2 * ny, RANK, width), BF16),
        1 << 32,
        8 << 20,
        sums,
    )
    panel = lax.all_to_all(panel, ("core", "y"), 0, 0)
    partial = kernel_call(
        next_sketch,
        shape((nx, RANK, rows), F32),
        flops,
        5 << 20,
        panel,
        transport,
    )
    parts = lax.all_to_all(partial, "x", 0, 0)

    sums, sketch = kernel_call(
        last_product,
        (shape((2, 8 * chips + 8, 128), F32), shape((RANK, rows), F32)),
        flops,
        6 << 20,
        parts,
        transport,
    )
    sums = lax.all_to_all(sums, "core", 0, 0)
    sums = kernel_call(add_cores, shape((chips, 24, 128), BF16), 0, 1 << 20, sums)
    sums = lax.all_to_all(sums, ("z", "y"), 0, 0)
    basis, coimage = kernel_call(
        functools.partial(finish, total_rows),
        (shape((RANK, rows), F32), shape((RANK, RANK), F32)),
        1 << 20,
        1 << 20,
        sums,
        sketch,
    )
    return (basis.T, coimage)


def solution(mesh):
    sizes = {"cam": (("y", 8), ("z", 8), ("core", 2)), "proj": (("x", 4),)}
    names = [name for axis in mesh.axis_names for name, _ in sizes[axis]]
    shape = [size for axis in mesh.axis_names for _, size in sizes[axis]]
    fine = Mesh(np.asarray(mesh.devices).reshape(shape), names)
    rows = ("y", "z", "core")
    return jax.shard_map(
        on_device,
        mesh=fine,
        in_specs=(P(rows, "x"), P(("x",) + rows, None)),
        out_specs=(P(rows, None), P(("x",) + rows, None)),
        check_vma=False,
    )
```

```python
import functools

import jax
import jax.numpy as jnp
import numpy as np
from jax import lax
from jax.experimental import pallas as pl
from jax.experimental.pallas import tpu as pltpu
from jax.sharding import Mesh
from jax.sharding import PartitionSpec as P

CHIPS = ("y", "z")
RANK = 32
HIGHEST = lax.Precision.HIGHEST
F32 = jnp.float32
BF16 = jnp.bfloat16
VMEM = pl.BlockSpec(memory_space=pltpu.VMEM)
NT = (((1,), (1,)), ((), ()))
TN = (((0,), (0,)), ((), ()))


def kernel_call(body, outs, flops, moved, *args):
    return pl.pallas_call(
        body,
        out_shape=outs,
        in_specs=[VMEM] * len(args),
        out_specs=jax.tree.map(lambda _: VMEM, outs),
        compiler_params=pltpu.CompilerParams(vmem_limit_bytes=24 << 20),
        cost_estimate=pl.CostEstimate(flops=flops, bytes_accessed=moved, transcendentals=0),
    )(*args)


def lanes_of(shape):
    return lax.broadcasted_iota(jnp.int32, shape, len(shape) - 1)


def pack_square(square):
    lane = lanes_of((8, 128))
    out = jnp.where(lane < 32, square[0:8], 0.0)
    for q in range(1, 4):
        block = pltpu.roll(square[8 * q : 8 * q + 8], 32 * q, axis=1)
        out = jnp.where((lane >= 32 * q) & (lane < 32 * q + 32), block, out)
    return out


def unpack_square(tile):
    return jnp.concatenate([tile] + [pltpu.roll(tile, 128 - 32 * q, axis=1) for q in range(1, 4)])


def pack_lower(square):
    lane = lanes_of((8, 128))
    out = jnp.where(lane < 32, square[24:32], 0.0)
    for at, width, first in ((32, 24, 16), (56, 16, 8), (72, 8, 0)):
        block = pltpu.roll(square[first : first + 8], at, axis=1)
        out = jnp.where((lane >= at) & (lane < at + width), block, out)
    return out


def unpack_lower(tile):
    lower = jnp.concatenate([pltpu.roll(tile, 128 - at, axis=1) for at in (72, 56, 32)] + [tile])
    lane = lanes_of((RANK, 128))
    row = lax.broadcasted_iota(jnp.int32, (RANK, 128), 0)
    lower = jnp.where(lane <= row, lower, 0.0)
    turned = jnp.concatenate([lower, jnp.zeros((128 - RANK, 128), F32)]).T[:RANK]
    return jnp.where(lane <= row, lower, turned)


def inverse_factor(gram):
    lane = lanes_of((RANK, 128))
    row = lax.broadcasted_iota(jnp.int32, (RANK, 128), 0)
    work = jnp.where(lane < RANK, gram, jnp.where(lane == row + RANK, 1.0, 0.0))
    pivots = jnp.ones((RANK, 128), F32)
    width = 16
    for start in range(0, RANK, width):
        columns = [
            jnp.broadcast_to(work[:, start + i : start + i + 1], (RANK, 128)) for i in range(width)
        ]
        for i in range(width):
            k = start + i
            pivot = jnp.broadcast_to(columns[i][k : k + 1], (RANK, 128))
            pivots = jnp.where(row == k, pivot, pivots)
            factor = jnp.where(row > k, columns[i] / pivot, 0.0)
            for later in range(i + 1, width):
                columns[later] = columns[later] - factor * columns[later][k : k + 1]
            work = work - factor * work[k : k + 1]
    return (work / jnp.sqrt(pivots))[:, RANK : 2 * RANK]


def fan_out(panel_ref, out_ref):
    panel = jnp.concatenate([panel_ref[...].astype(F32), jnp.zeros((RANK, 128 - RANK), F32)], axis=1)
    tile = pack_square(panel).astype(BF16)
    for copy in range(out_ref.shape[0]):
        out_ref[copy] = tile


def first_sketch(tiles_ref, transport_ref, out_ref):
    cores, chips = tiles_ref.shape[:2]
    cols = transport_ref.shape[1]
    lane = lanes_of((8, 128))
    masks = [(lane >= 32 * q) & (lane < 32 * q + 32) for q in range(4)]
    total = jnp.zeros((transport_ref.shape[0], 128), F32)
    group = 8
    for start in range(0, chips, group):
        rows = []
        for chip in range(start, start + group):
            for core in range(cores):
                tile = tiles_ref[core, chip].astype(F32)
                rows += [jnp.where(mask, tile, 0.0) for mask in masks]
        at = start * (cols // chips)
        total += jnp.dot(
            transport_ref[:, at : at + group * (cols // chips)],
            jnp.concatenate(rows).astype(BF16),
            preferred_element_type=F32,
        )
    turned = total.T
    sketch = (turned[0:32] + turned[32:64]) + (turned[64:96] + turned[96:128])
    for copy in range(out_ref.shape[0]):
        out_ref[copy] = sketch


def next_sketch(panel_ref, transport_ref, out_ref):
    groups, _, width = panel_ref.shape
    sketch = jnp.zeros((RANK, transport_ref.shape[0]), F32)
    for g in range(groups):
        sketch += lax.dot_general(
            panel_ref[g],
            transport_ref[:, g * width : (g + 1) * width],
            NT,
            preferred_element_type=F32,
        )
    for copy in range(out_ref.shape[0]):
        out_ref[copy] = sketch


def product(parts_ref, transport_ref):
    sketch = (parts_ref[0] + parts_ref[1]) + (parts_ref[2] + parts_ref[3])
    gram = lax.dot_general(sketch, sketch, NT, precision=HIGHEST, preferred_element_type=F32)
    gram = jnp.concatenate([gram, jnp.zeros((RANK, 128 - RANK), F32)], axis=1)
    high = sketch.astype(BF16)
    low = (sketch - high.astype(F32)).astype(BF16)
    both = jnp.concatenate([high, low])

    def columns(at, width):
        out = jnp.dot(both, transport_ref[:, at : at + width], preferred_element_type=F32)
        return out[:RANK] + out[RANK:]

    return sketch, pack_lower(gram), columns


def middle_product(parts_ref, transport_ref, out_ref):
    groups, height, _ = out_ref.shape
    width = transport_ref.shape[1] // groups
    _, gram, columns = product(parts_ref, transport_ref)
    gram = three_terms(gram)
    for group in range(groups):
        block = columns(group * width, width)
        tiles = [block[:, 128 * c : 128 * c + 128] for c in range(width // 128)]
        out_ref[group] = jnp.concatenate(tiles + [gram]).astype(BF16)


def last_product(parts_ref, transport_ref, out_ref, sketch_ref):
    cores, height, _ = out_ref.shape
    chips = height // 8 - 1
    sketch, gram, columns = product(parts_ref, transport_ref)
    sketch_ref[...] = sketch
    lane = lanes_of((8, 128))
    low_half, even = lane < 64, lane % 64 < 32
    for wide in range(chips // 8):
        block = columns(512 * wide, 512)
        for c in range(4):
            t = [block[8 * a : 8 * a + 8, 128 * c : 128 * c + 128] for a in range(4)]
            u = [None] * 4
            for a in (0, 1):
                u[a] = jnp.where(low_half, t[a], pltpu.roll(t[a + 2], 64, axis=1))
                u[a + 2] = jnp.where(low_half, pltpu.roll(t[a], 64, axis=1), t[a + 2])
            for a in (0, 2):
                v0 = jnp.where(even, u[a], pltpu.roll(u[a + 1], 32, axis=1))
                v1 = jnp.where(even, pltpu.roll(u[a], 96, axis=1), u[a + 1])
                for b, v in ((a, v0), (a + 1, v1)):
                    device = 16 * wide + 4 * c + b
                    y, z = divmod(device // 2, 8)
                    at = 8 * (z * (chips // 8) + y)
                    out_ref[device % 2, at : at + 8] = v
    for core in range(cores):
        out_ref[core, height - 8 : height] = gram


def three_terms(gram):
    lane = lanes_of((8, 128))
    terms = []
    for _ in range(3):
        terms.append(gram.astype(BF16).astype(F32))
        gram = gram - terms[-1]
    middle = pltpu.roll(terms[1], 80, axis=1)
    first = jnp.where(lane < 80, terms[0], middle)
    second = jnp.where(lane < 32, middle, pltpu.roll(terms[2], 32, axis=1))
    return jnp.concatenate([first, second])


def decoded_sum(messages_ref):
    total = messages_ref[0].astype(F32)
    for p in range(1, messages_ref.shape[0]):
        total = total + messages_ref[p].astype(F32)
    lane = lanes_of((8, 128))
    first, second = total[-16:-8], total[-8:]
    middle = pltpu.roll(jnp.where(lane < 32, second, first), 48, axis=1)
    gram = (pltpu.roll(second, 96, axis=1) + middle) + first
    return jnp.concatenate([total[:-16], jnp.where(lane < 80, gram, 0.0)])


def add_cores(sums_ref, out_ref):
    peers, height, _ = out_ref.shape
    rows = height - 16
    gram = three_terms(sums_ref[0, peers * rows :] + sums_ref[1, peers * rows :])
    for peer in range(peers):
        at = slice(peer * rows, (peer + 1) * rows)
        block = sums_ref[0, at] + sums_ref[1, at]
        out_ref[peer] = jnp.concatenate([block, gram]).astype(BF16)


def add_peers(messages_ref, out_ref):
    total = decoded_sum(messages_ref)
    message = jnp.concatenate([total[:-8], three_terms(total[-8:])]).astype(BF16)
    for copy in range(out_ref.shape[0]):
        out_ref[copy] = message


def normalise(total_rows, messages_ref, out_ref):
    total = decoded_sum(messages_ref)
    tiles = total.shape[0] // 8 - 1
    inverse = inverse_factor(unpack_lower(total[8 * tiles :]) / total_rows)
    for c in range(tiles // 4):
        block = total[32 * c : 32 * c + 32]
        panel = jnp.dot(inverse, block, precision=HIGHEST, preferred_element_type=F32).astype(BF16)
        for copy in range(out_ref.shape[0]):
            out_ref[copy, :, 128 * c : 128 * c + 128] = panel


def finish(total_rows, messages_ref, sketch_ref, basis_ref, coimage_ref):
    total = decoded_sum(messages_ref)
    inverse = inverse_factor(unpack_lower(total[8:]) / total_rows)
    basis_ref[...] = jnp.dot(
        inverse, sketch_ref[...], precision=HIGHEST, preferred_element_type=F32
    )
    block = unpack_square(total[0:8])[:, :RANK]
    coimage_ref[...] = lax.dot_general(
        block, inverse, (((0,), (1,)), ((), ())), precision=HIGHEST, preferred_element_type=F32
    )


def on_device(transport, test_panel):
    rows, cols = transport.shape
    total_rows = rows * lax.axis_size(("y", "z", "core"))
    ny, nz, nx = (lax.axis_size(name) for name in ("y", "z", "x"))
    chips = ny * nz
    flops = 2 * rows * cols * 128
    shape = jax.ShapeDtypeStruct

    copies = kernel_call(fan_out, shape((chips, 8, 128), BF16), 1 << 32, 8 << 20, test_panel)
    tiles = lax.all_to_all(copies, CHIPS, 0, 0)
    tiles = lax.all_to_all(jnp.broadcast_to(tiles, (2, chips, 8, 128)), "core", 0, 0)
    partial = kernel_call(
        first_sketch, shape((nx, RANK, rows), F32), flops, 5 << 20, tiles, transport
    )
    parts = lax.all_to_all(partial, "x", 0, 0)

    width = cols // (2 * ny)
    height = RANK * width // 128
    sums = kernel_call(
        middle_product, shape((2 * ny, height + 16, 128), BF16), flops, 5 << 20, parts, transport
    )
    sums = lax.all_to_all(sums, ("core", "y"), 0, 0)
    sums = kernel_call(add_peers, shape((nz, height + 16, 128), BF16), 0, 1 << 20, sums)
    sums = lax.all_to_all(sums, "z", 0, 0)
    panel = kernel_call(
        functools.partial(normalise, total_rows),
        shape((2 * ny, RANK, width), BF16),
        1 << 32,
        8 << 20,
        sums,
    )
    panel = lax.all_to_all(panel, ("core", "y"), 0, 0)
    partial = kernel_call(
        next_sketch,
        shape((nx, RANK, rows), F32),
        flops,
        5 << 20,
        panel,
        transport,
    )
    parts = lax.all_to_all(partial, "x", 0, 0)

    sums, sketch = kernel_call(
        last_product,
        (shape((2, 8 * chips + 8, 128), F32), shape((RANK, rows), F32)),
        flops,
        6 << 20,
        parts,
        transport,
    )
    sums = lax.all_to_all(sums, "core", 0, 0)
    sums = kernel_call(add_cores, shape((chips, 24, 128), BF16), 0, 1 << 20, sums)
    sums = lax.all_to_all(sums, ("z", "y"), 0, 0)
    basis, coimage = kernel_call(
        functools.partial(finish, total_rows),
        (shape((RANK, rows), F32), shape((RANK, RANK), F32)),
        1 << 20,
        1 << 20,
        sums,
        sketch,
    )
    return (basis.T, coimage)


def solution(mesh):
    sizes = {"cam": (("y", 8), ("z", 8), ("core", 2)), "proj": (("x", 4),)}
    names = [name for axis in mesh.axis_names for name, _ in sizes[axis]]
    shape = [size for axis in mesh.axis_names for _, size in sizes[axis]]
    fine = Mesh(np.asarray(mesh.devices).reshape(shape), names)
    rows = ("y", "z", "core")
    return jax.shard_map(
        on_device,
        mesh=fine,
        in_specs=(P(rows, "x"), P(("x",) + rows, None)),
        out_specs=(P(rows, None), P(("x",) + rows, None)),
        check_vma=False,
    )
```

```python
import functools

import jax
import jax.numpy as jnp
import numpy as np
from jax import lax
from jax.experimental import pallas as pl
from jax.experimental.pallas import tpu as pltpu
from jax.sharding import Mesh
from jax.sharding import PartitionSpec as P

CHIPS = ("y", "z")
RANK = 32
HIGHEST = lax.Precision.HIGHEST
F32 = jnp.float32
BF16 = jnp.bfloat16
VMEM = pl.BlockSpec(memory_space=pltpu.VMEM)
NT = (((1,), (1,)), ((), ()))
TN = (((0,), (0,)), ((), ()))


def kernel_call(body, outs, flops, moved, *args):
    return pl.pallas_call(
        body,
        out_shape=outs,
        in_specs=[VMEM] * len(args),
        out_specs=jax.tree.map(lambda _: VMEM, outs),
        compiler_params=pltpu.CompilerParams(vmem_limit_bytes=24 << 20),
        cost_estimate=pl.CostEstimate(flops=flops, bytes_accessed=moved, transcendentals=0),
    )(*args)


def lanes_of(shape):
    return lax.broadcasted_iota(jnp.int32, shape, len(shape) - 1)


def pack_square(square):
    lane = lanes_of((8, 128))
    out = jnp.where(lane < 32, square[0:8], 0.0)
    for q in range(1, 4):
        block = pltpu.roll(square[8 * q : 8 * q + 8], 32 * q, axis=1)
        out = jnp.where((lane >= 32 * q) & (lane < 32 * q + 32), block, out)
    return out


def unpack_square(tile):
    return jnp.concatenate([tile] + [pltpu.roll(tile, 128 - 32 * q, axis=1) for q in range(1, 4)])


def pack_lower(square):
    lane = lanes_of((8, 128))
    out = jnp.where(lane < 32, square[24:32], 0.0)
    for at, width, first in ((32, 24, 16), (56, 16, 8), (72, 8, 0)):
        block = pltpu.roll(square[first : first + 8], at, axis=1)
        out = jnp.where((lane >= at) & (lane < at + width), block, out)
    return out


def unpack_lower(tile):
    lower = jnp.concatenate([pltpu.roll(tile, 128 - at, axis=1) for at in (72, 56, 32)] + [tile])
    lane = lanes_of((RANK, 128))
    row = lax.broadcasted_iota(jnp.int32, (RANK, 128), 0)
    lower = jnp.where(lane <= row, lower, 0.0)
    turned = jnp.concatenate([lower, jnp.zeros((128 - RANK, 128), F32)]).T[:RANK]
    return jnp.where(lane <= row, lower, turned)


def inverse_factor(gram):
    lane = lanes_of((RANK, 128))
    row = lax.broadcasted_iota(jnp.int32, (RANK, 128), 0)
    work = jnp.where(lane < RANK, gram, jnp.where(lane == row + RANK, 1.0, 0.0))
    pivots = jnp.ones((RANK, 128), F32)
    width = 16
    for start in range(0, RANK, width):
        columns = [
            jnp.broadcast_to(work[:, start + i : start + i + 1], (RANK, 128)) for i in range(width)
        ]
        for i in range(width):
            k = start + i
            pivot = jnp.broadcast_to(columns[i][k : k + 1], (RANK, 128))
            pivots = jnp.where(row == k, pivot, pivots)
            factor = jnp.where(row > k, columns[i] / pivot, 0.0)
            for later in range(i + 1, width):
                columns[later] = columns[later] - factor * columns[later][k : k + 1]
            work = work - factor * work[k : k + 1]
    return (work / jnp.sqrt(pivots))[:, RANK : 2 * RANK]


def fan_out(panel_ref, out_ref):
    panel = jnp.concatenate([panel_ref[...].astype(F32), jnp.zeros((RANK, 128 - RANK), F32)], axis=1)
    tile = pack_square(panel).astype(BF16)
    for copy in range(out_ref.shape[0]):
        out_ref[copy] = tile


def first_sketch(tiles_ref, transport_ref, out_ref):
    cores, chips = tiles_ref.shape[:2]
    cols = transport_ref.shape[1]
    lane = lanes_of((8, 128))
    masks = [(lane >= 32 * q) & (lane < 32 * q + 32) for q in range(4)]
    total = jnp.zeros((transport_ref.shape[0], 128), F32)
    group = 8
    for start in range(0, chips, group):
        rows = []
        for chip in range(start, start + group):
            for core in range(cores):
                tile = tiles_ref[core, chip].astype(F32)
                rows += [jnp.where(mask, tile, 0.0) for mask in masks]
        at = start * (cols // chips)
        total += jnp.dot(
            transport_ref[:, at : at + group * (cols // chips)],
            jnp.concatenate(rows).astype(BF16),
            preferred_element_type=F32,
        )
    turned = total.T
    sketch = (turned[0:32] + turned[32:64]) + (turned[64:96] + turned[96:128])
    for copy in range(out_ref.shape[0]):
        out_ref[copy] = sketch


def next_sketch(panel_ref, transport_ref, out_ref):
    groups, _, width = panel_ref.shape
    sketch = jnp.zeros((RANK, transport_ref.shape[0]), F32)
    for g in range(groups):
        sketch += lax.dot_general(
            panel_ref[g],
            transport_ref[:, g * width : (g + 1) * width],
            NT,
            preferred_element_type=F32,
        )
    for copy in range(out_ref.shape[0]):
        out_ref[copy] = sketch


def product(parts_ref, transport_ref):
    sketch = (parts_ref[0] + parts_ref[1]) + (parts_ref[2] + parts_ref[3])
    gram = lax.dot_general(sketch, sketch, NT, precision=HIGHEST, preferred_element_type=F32)
    gram = jnp.concatenate([gram, jnp.zeros((RANK, 128 - RANK), F32)], axis=1)
    high = sketch.astype(BF16)
    low = (sketch - high.astype(F32)).astype(BF16)
    both = jnp.concatenate([high, low])

    def columns(at, width):
        out = jnp.dot(both, transport_ref[:, at : at + width], preferred_element_type=F32)
        return out[:RANK] + out[RANK:]

    return sketch, pack_lower(gram), columns


def middle_product(parts_ref, transport_ref, out_ref):
    groups, height, _ = out_ref.shape
    width = transport_ref.shape[1] // groups
    _, gram, columns = product(parts_ref, transport_ref)
    gram = three_terms(gram)
    for group in range(groups):
        block = columns(group * width, width)
        tiles = [block[:, 128 * c : 128 * c + 128] for c in range(width // 128)]
        out_ref[group] = jnp.concatenate(tiles + [gram]).astype(BF16)


def last_product(parts_ref, transport_ref, out_ref, sketch_ref):
    chips = out_ref.shape[0] * 4
    sketch, gram, columns = product(parts_ref, transport_ref)
    sketch_ref[...] = sketch
    lane = lanes_of((8, 128))
    low_half, even = lane < 64, lane % 64 < 32
    for wide in range(chips // 8):
        block = columns(512 * wide, 512)
        for c in range(4):
            t = [block[8 * a : 8 * a + 8, 128 * c : 128 * c + 128] for a in range(4)]
            u = [None] * 4
            for a in (0, 1):
                u[a] = jnp.where(low_half, t[a], pltpu.roll(t[a + 2], 64, axis=1))
                u[a + 2] = jnp.where(low_half, pltpu.roll(t[a], 64, axis=1), t[a + 2])
            for a in (0, 2):
                v0 = jnp.where(even, u[a], pltpu.roll(u[a + 1], 32, axis=1))
                v1 = jnp.where(even, pltpu.roll(u[a], 96, axis=1), u[a + 1])
                for b, v in ((a, v0), (a + 1, v1)):
                    device = 16 * wide + 4 * c + b
                    y, z = divmod(device // 2, 8)
                    out_ref[device % 2 * 8 + y, 8 * z : 8 * z + 8] = v.astype(BF16)
    gram = three_terms(gram).astype(BF16)
    for group in range(out_ref.shape[0]):
        out_ref[group, 64:80] = gram


def three_terms(gram):
    lane = lanes_of((8, 128))
    terms = []
    for _ in range(3):
        terms.append(gram.astype(BF16).astype(F32))
        gram = gram - terms[-1]
    middle = pltpu.roll(terms[1], 80, axis=1)
    first = jnp.where(lane < 80, terms[0], middle)
    second = jnp.where(lane < 32, middle, pltpu.roll(terms[2], 32, axis=1))
    return jnp.concatenate([first, second])


def decoded_sum(messages_ref):
    total = messages_ref[0].astype(F32)
    for p in range(1, messages_ref.shape[0]):
        total = total + messages_ref[p].astype(F32)
    lane = lanes_of((8, 128))
    first, second = total[-16:-8], total[-8:]
    middle = pltpu.roll(jnp.where(lane < 32, second, first), 48, axis=1)
    gram = (pltpu.roll(second, 96, axis=1) + middle) + first
    return jnp.concatenate([total[:-16], jnp.where(lane < 80, gram, 0.0)])


def split_tiles(messages_ref, out_ref):
    total = decoded_sum(messages_ref)
    gram = three_terms(total[-8:])
    for z in range(out_ref.shape[0]):
        tile = total[8 * z : 8 * z + 8]
        high = tile.astype(BF16).astype(F32)
        out_ref[z] = jnp.concatenate([high, tile - high, gram]).astype(BF16)


def add_peers(messages_ref, out_ref):
    total = decoded_sum(messages_ref)
    message = jnp.concatenate([total[:-8], three_terms(total[-8:])]).astype(BF16)
    for copy in range(out_ref.shape[0]):
        out_ref[copy] = message


def normalise(total_rows, messages_ref, out_ref):
    total = decoded_sum(messages_ref)
    tiles = total.shape[0] // 8 - 1
    inverse = inverse_factor(unpack_lower(total[8 * tiles :]) / total_rows)
    for c in range(tiles // 4):
        block = total[32 * c : 32 * c + 32]
        panel = jnp.dot(inverse, block, precision=HIGHEST, preferred_element_type=F32).astype(BF16)
        for copy in range(out_ref.shape[0]):
            out_ref[copy, :, 128 * c : 128 * c + 128] = panel


def finish(total_rows, messages_ref, sketch_ref, basis_ref, coimage_ref):
    total = decoded_sum(messages_ref)
    inverse = inverse_factor(unpack_lower(total[16:]) / total_rows)
    basis_ref[...] = jnp.dot(
        inverse, sketch_ref[...], precision=HIGHEST, preferred_element_type=F32
    )
    block = unpack_square(total[0:8] + total[8:16])[:, :RANK]
    coimage_ref[...] = lax.dot_general(
        block, inverse, (((0,), (1,)), ((), ())), precision=HIGHEST, preferred_element_type=F32
    )


def on_device(transport, test_panel):
    rows, cols = transport.shape
    total_rows = rows * lax.axis_size(("y", "z", "core"))
    ny, nz, nx = (lax.axis_size(name) for name in ("y", "z", "x"))
    chips = ny * nz
    flops = 2 * rows * cols * 128
    shape = jax.ShapeDtypeStruct

    copies = kernel_call(fan_out, shape((chips, 8, 128), BF16), 1 << 32, 8 << 20, test_panel)
    tiles = lax.all_to_all(copies, CHIPS, 0, 0)
    tiles = lax.all_to_all(jnp.broadcast_to(tiles, (2, chips, 8, 128)), "core", 0, 0)
    partial = kernel_call(
        first_sketch, shape((nx, RANK, rows), F32), flops, 5 << 20, tiles, transport
    )
    parts = lax.all_to_all(partial, "x", 0, 0)

    width = cols // (2 * ny)
    height = RANK * width // 128
    sums = kernel_call(
        middle_product, shape((2 * ny, height + 16, 128), BF16), flops, 5 << 20, parts, transport
    )
    sums = lax.all_to_all(sums, ("core", "y"), 0, 0)
    sums = kernel_call(add_peers, shape((nz, height + 16, 128), BF16), 0, 1 << 20, sums)
    sums = lax.all_to_all(sums, "z", 0, 0)
    panel = kernel_call(
        functools.partial(normalise, total_rows),
        shape((2 * ny, RANK, width), BF16),
        1 << 32,
        8 << 20,
        sums,
    )
    panel = lax.all_to_all(panel, ("core", "y"), 0, 0)
    partial = kernel_call(
        next_sketch,
        shape((nx, RANK, rows), F32),
        flops,
        5 << 20,
        panel,
        transport,
    )
    parts = lax.all_to_all(partial, "x", 0, 0)

    sums, sketch = kernel_call(
        last_product,
        (shape((2 * ny, 8 * nz + 16, 128), BF16), shape((RANK, rows), F32)),
        flops,
        6 << 20,
        parts,
        transport,
    )
    sums = lax.all_to_all(sums, ("core", "y"), 0, 0)
    sums = kernel_call(split_tiles, shape((nz, 32, 128), BF16), 0, 1 << 20, sums)
    sums = lax.all_to_all(sums, "z", 0, 0)
    basis, coimage = kernel_call(
        functools.partial(finish, total_rows),
        (shape((RANK, rows), F32), shape((RANK, RANK), F32)),
        1 << 20,
        1 << 20,
        sums,
        sketch,
    )
    return (basis.T, coimage)


def solution(mesh):
    sizes = {"cam": (("y", 8), ("z", 8), ("core", 2)), "proj": (("x", 4),)}
    names = [name for axis in mesh.axis_names for name, _ in sizes[axis]]
    shape = [size for axis in mesh.axis_names for _, size in sizes[axis]]
    fine = Mesh(np.asarray(mesh.devices).reshape(shape), names)
    rows = ("y", "z", "core")
    return jax.shard_map(
        on_device,
        mesh=fine,
        in_specs=(P(rows, "x"), P(("x",) + rows, None)),
        out_specs=(P(rows, None), P(("x",) + rows, None)),
        check_vma=False,
    )
```
